128 devices in a mesh: seq: 8 (over x_lo, z), fft: 16 (over y, x_hi, core).
Axes of the slice: x: 4 (x_hi: 2, x_lo: 2; x = x_hi * 2 + x_lo), y: 4, z: 4, core: 2. Of those that a mesh axis runs over, the one named last changes fastest.
Arguments:
- features: bfloat16 [256, 16384], P(None, ('seq', 'fft')), may hold values from -6 to 6
- sink_order: int32 [128, 128], P(('seq', 'fft')), may hold values from 0 to 127, each once within a row
- cotangent: bfloat16 [256, 16384], P(None, ('seq', 'fft')), may hold values from -6 to 6
- w_in: bfloat16 [768, 256], replicated, may hold values from -0.375 to 0.375
- short_taps: float32 [768, 3], replicated, may hold values from -1 to 1
- w_out: bfloat16 [256, 256], replicated, may hold values from -0.375 to 0.375
- filter_one: float32 [256, 16384], P(('seq', 'fft')), may hold values from -2 to 2
- filter_two: float32 [256, 16384], P(('seq', 'fft')), may hold values from -2 to 2
Outputs:
- grad_features: bfloat16 [256, 16384], P(None, ('seq', 'fft'))
- grad_w_in: float32 [768, 256], replicated
- grad_w_out: float32 [256, 256], replicated
- grad_short: float32 [768, 3], replicated
- grad_filter_one: float32 [256, 16384], P(('seq', 'fft'))
- grad_filter_two: float32 [256, 16384], P(('seq', 'fft'))
The draws below stay inside these ranges and needn't reach their ends.
Inputs may be any that keep to these rules, and one draw needn't show every extreme that they name: Each row of sink_order names every position of a block of 128 sinks once.
All inputs are finite; a program needn't handle non-finite values.
Results may differ from the reference program's by a relative error of at most 0.0089.
Values may be sent and summed in bfloat16 or wider, within the bound.
A program may use at most 64 MiB of HBM per device.

```python
import math
import jax
import jax.numpy as jnp
from jax import lax

D = 256
ROWS_DEV = 128
BLOCKS = 128
SINKS = 16384


def filter_draw(key, salt):
    key = jax.random.fold_in(key, salt)
    keys = jax.random.split(key, 6)
    sample_location = jnp.arange(SINKS, dtype=jnp.float32)[None, :]
    share = 0.5
    slow = jax.random.uniform(keys[0], (D, 1), dtype=jnp.float32) < share
    slow_rate = jnp.exp(jax.random.uniform(keys[1], (D, 1), dtype=jnp.float32, minval=math.log(0.2 / SINKS), maxval=math.log(2.0 / SINKS)))
    fast_rate = jnp.exp(jax.random.uniform(keys[2], (D, 1), dtype=jnp.float32, minval=math.log(1.0 / 50.0), maxval=math.log(1.0 / 20.0)))
    decay = jnp.where(slow, slow_rate, fast_rate)
    decay_profile = jnp.exp(-decay * sample_location)
    sample_points = jax.random.uniform(keys[3], (D, 3), dtype=jnp.float32) * SINKS
    delay_losses = jax.random.uniform(keys[4], (D, 3), dtype=jnp.float32, minval=0.5, maxval=0.8)
    for pulse_train in range(3):
        decay_profile = decay_profile * jnp.where(sample_location >= sample_points[:, pulse_train:pulse_train + 1], delay_losses[:, pulse_train:pulse_train + 1], 1.0)
    gain_factor = jnp.sqrt(-jnp.expm1(-2.0 * decay))
    noise = jax.random.uniform(keys[5], (D, SINKS), dtype=jnp.float32, minval=-1.7, maxval=1.7)
    return (noise * decay_profile * gain_factor).astype(jnp.float32)


def draw_filter_one(key, part):
    return filter_draw(key, 11)


def draw_filter_two(key, part):
    return filter_draw(key, 23)


def steps_of(rng, extent, cuts, smallest, largest):
    factor_of, own = 1.0, jax.random.fold_in(rng, 6)
    for position, shards_of in cuts:
        heights = jnp.exp(jax.random.uniform(jax.random.fold_in(own, position), (shards_of,), jnp.float32, smallest / len(cuts), largest / len(cuts)))
        factor_of = factor_of * jnp.repeat(heights, extent[position] // shards_of).reshape([-1 if axis == position else 1 for axis in range(len(extent))])
    return factor_of


def centred(stream_key, shape, deviation, most, cuts=(), kind=jnp.bfloat16):
    level = steps_of(stream_key, shape, cuts, -0.22, 0.18) if cuts else 1.0
    values = jax.random.normal(stream_key, shape, jnp.float32) * deviation * level
    return jnp.minimum(jnp.maximum(values, -most), most).astype(kind)


def setup_inputs(seed: int = 0) -> dict:
    splits = jax.random.split(jax.random.key(seed), 9)
    features = centred(splits[0], (D, SINKS), 1.0, 6.0, ((1, 128),))
    sink_order = jax.vmap(lambda own: jax.random.permutation(own, ROWS_DEV))(jax.random.split(splits[1], BLOCKS)).reshape((BLOCKS, ROWS_DEV)).astype(jnp.int32)
    cotangent = centred(splits[2], (D, SINKS), 1.0, 6.0, ((1, 128),))
    w_in = centred(splits[3], (3 * D, D), D ** -0.5, 0.375)
    short_taps = jnp.clip(jax.random.uniform(splits[4], (3 * D, 3), jnp.float32, -1.0, 1.0), -1.0, 1.0)
    w_out = centred(splits[5], (D, D), D ** -0.5, 0.375)
    filter_one = draw_filter_one(jax.random.fold_in(splits[8], 71), 0)
    filter_two = draw_filter_two(jax.random.fold_in(splits[8], 71), 0)
    return dict(features=features, sink_order=sink_order, cotangent=cotangent, w_in=w_in, short_taps=short_taps, w_out=w_out, filter_one=filter_one, filter_two=filter_two)


def long_conv(filt, signal):
    total = 2 * SINKS
    spec_a = jnp.fft.rfft(filt, n=total, axis=1)
    spec_b = jnp.fft.rfft(signal, n=total, axis=1)
    return jnp.fft.irfft(spec_a * spec_b, n=total, axis=1)[:, :SINKS]

def long_corr(first, second):
    total = 2 * SINKS
    spec_a = jnp.fft.rfft(first, n=total, axis=1)
    spec_b = jnp.fft.rfft(second, n=total, axis=1)
    return jnp.fft.irfft(jnp.conj(spec_a) * spec_b, n=total, axis=1)[:, :SINKS]

def reference(features, sink_order, cotangent, w_in, short_taps, w_out, filter_one, filter_two):
    scale = 1.0 / math.sqrt(SINKS)
    block_ids = jnp.arange(BLOCKS, dtype=jnp.int32)[:, None] * jnp.ones((1, ROWS_DEV), jnp.int32)
    order = sink_order.astype(jnp.int32)
    feat_blocks = features.reshape(D, BLOCKS, ROWS_DEV)
    seq_input = feat_blocks[:, block_ids, order].reshape(D, SINKS)
    projected = jnp.dot(w_in, seq_input, preferred_element_type=jnp.float32)
    padded = jnp.pad(projected, ((0, 0), (2, 0)))
    mixed = short_taps[:, 0:1] * padded[:, 2:2 + SINKS]
    for offset in range(1, 3):
        mixed = mixed + short_taps[:, offset:offset + 1] * padded[:, 2 - offset:2 - offset + SINKS]
    streams = mixed.astype(jnp.bfloat16)
    value = streams[:D].astype(jnp.float32)
    gate_one = streams[D:2 * D].astype(jnp.float32)
    gate_two = streams[2 * D:].astype(jnp.float32)
    out_grad = jnp.dot(w_out.T, cotangent, preferred_element_type=jnp.float32).astype(jnp.bfloat16)
    out_gradf = out_grad.astype(jnp.float32)
    first_mix = long_conv(filter_one, value)
    first_out = gate_one * first_mix
    second_mix = long_conv(filter_two, first_out)
    second_out = (gate_two * second_mix).astype(jnp.bfloat16)
    grad_gate_two = (out_gradf * second_mix).astype(jnp.bfloat16)
    grad_second_mix = out_gradf * gate_two
    grad_first_out = long_corr(filter_two, grad_second_mix)
    grad_filter_two = long_corr(first_out, grad_second_mix) * scale
    grad_gate_one = (grad_first_out * first_mix).astype(jnp.bfloat16)
    grad_first_mix = grad_first_out * gate_one
    grad_value = long_corr(filter_one, grad_first_mix).astype(jnp.bfloat16)
    grad_filter_one = long_corr(value, grad_first_mix) * scale
    grad_streams = jnp.concatenate([grad_value, grad_gate_one, grad_gate_two], axis=0)
    grad_padded = jnp.pad(grad_streams, ((0, 0), (0, 2)))
    grad_mixed = short_taps[:, 0:1] * grad_padded[:, 0:SINKS]
    for offset in range(1, 3):
        grad_mixed = grad_mixed + short_taps[:, offset:offset + 1] * grad_padded[:, offset:offset + SINKS]
    grad_projected = grad_mixed.astype(jnp.bfloat16)
    grad_streamsf = grad_streams.astype(jnp.float32)
    tap_terms = []
    for offset in range(3):
        tap_terms.append(lax.optimization_barrier(jnp.sum(grad_streamsf * padded[:, 2 - offset:2 - offset + SINKS], axis=1)))
    grad_short = jnp.stack(tap_terms, axis=1) * scale
    grad_w_in = lax.dot_general(grad_projected, seq_input, (((1,), (1,)), ((), ())), preferred_element_type=jnp.float32) * scale
    grad_w_out = lax.dot_general(cotangent, second_out, (((1,), (1,)), ((), ())), preferred_element_type=jnp.float32) * scale
    grad_seq = lax.dot_general(w_in, grad_projected, (((0,), (0,)), ((), ())), preferred_element_type=jnp.float32).astype(jnp.bfloat16)
    grad_blocks = grad_seq.reshape(D, BLOCKS, ROWS_DEV)
    unordered = jnp.zeros_like(grad_blocks).at[:, block_ids, order].set(grad_blocks)
    grad_features = unordered.reshape(D, SINKS)
    return (grad_features, grad_w_in, grad_w_out, grad_short, grad_filter_one, grad_filter_two)
```

```python
import functools
import math

import jax
import jax.numpy as jnp
import ml_dtypes
import numpy as np
from jax import lax
from jax.experimental import pallas as pl
from jax.experimental.pallas import tpu as pltpu
from jax.sharding import PartitionSpec as P

bf16 = jnp.bfloat16
f32 = jnp.float32
LOGICAL = pl.DeviceIdType.LOGICAL


def table_halves(table):
    high = table.astype(ml_dtypes.bfloat16)
    low = (table - high.astype(np.float64)).astype(ml_dtypes.bfloat16)
    return high, low


def transform_tables(blocks, lanes):
    length = blocks * lanes
    shift = 0.25
    row = np.arange(blocks, dtype=np.float64)
    lane = np.arange(lanes, dtype=np.float64)
    outer = -2.0 * np.pi * np.outer(row + shift, row) / blocks
    twist = -2.0 * np.pi * np.outer(row + shift, lane) / length
    inner = -2.0 * np.pi * (np.outer(lane, lane) % lanes) / lanes
    first = np.concatenate([np.cos(outer), np.sin(outer)], axis=0)
    second = np.block(
        [[np.cos(inner), np.sin(inner)], [-np.sin(inner), np.cos(inner)]]
    )
    second_back = second.T
    first_back = np.concatenate([np.cos(outer).T, np.sin(outer).T], axis=1) / length
    twiddle = np.concatenate([np.cos(twist), np.sin(twist)], axis=1).astype(np.float32)
    return (
        *table_halves(first),
        *table_halves(second),
        *table_halves(second_back),
        *table_halves(first_back),
        twiddle,
    )


def halves(x):
    high = x.astype(bf16)
    return high, (x - high.astype(f32)).astype(bf16)


def dot(a, b):
    return jnp.dot(a, b, preferred_element_type=f32)


def dot_nt(a, b):
    return lax.dot_general(a, b, (((1,), (1,)), ((), ())), preferred_element_type=f32)


def dot_tn(a, b):
    return lax.dot_general(a, b, (((0,), (0,)), ((), ())), preferred_element_type=f32)


def dot3(left, right):
    return dot(left[0], right[0]) + (dot(left[0], right[1]) + dot(left[1], right[0]))


def kernel(
    count,
    fft_size,
    feat_ref,
    order_ref,
    cot_ref,
    win_ref,
    taps_ref,
    wout_ref,
    filt1_ref,
    filt2_ref,
    t1h,
    t1l,
    t2h,
    t2l,
    u2h,
    u2l,
    u1h,
    u1l,
    tw_ref,
    gfeat_ref,
    gwin_ref,
    gwout_ref,
    gshort_ref,
    gf1_ref,
    gf2_ref,
    stage_a,
    stage_b,
    seq_scr,
    send1,
    recv1,
    send2,
    recv2,
    send3,
    recv3,
    slab,
    recv4,
    short_slab,
    recv_short,
    send_sem,
    recv_sem,
):
    blocks = count
    lanes = 128
    width = 2 * count
    me = lax.axis_index("seq") * fft_size + lax.axis_index("fft")
    scale = 1.0 / math.sqrt(blocks * lanes)

    barrier = pltpu.get_barrier_semaphore()

    def greet(i, carry):
        pl.semaphore_signal(
            barrier, inc=1, device_id=lax.rem(me + i, count), device_id_type=LOGICAL
        )
        return carry

    lax.fori_loop(1, count, greet, 0)

    def exchange(source, target, phase):
        def one(i, carry):
            peer = lax.rem(me + i, count)
            pltpu.make_async_remote_copy(
                source(peer),
                target.at[me],
                send_sem.at[phase],
                recv_sem.at[phase],
                device_id=peer,
                device_id_type=LOGICAL,
            ).start()
            return carry

        lax.fori_loop(1, count, one, 0)
        pltpu.make_async_copy(source(me), target.at[me], recv_sem.at[phase]).start()

    def arrived(target, phase):
        pltpu.make_async_copy(target, target, recv_sem.at[phase]).wait()

    def sent(target, phase):
        part = target.at[pl.ds(0, count - 1)]
        pltpu.make_async_copy(part, part, send_sem.at[phase]).wait()

    order = order_ref[...]
    pick = jnp.where(
        lax.broadcasted_iota(jnp.int32, (lanes, lanes), 0) == order, 1.0, 0.0
    ).astype(bf16)
    seq_scr[...] = dot(feat_ref[...], pick).astype(bf16)
    stage_a[0 : 3 * width, :] = dot(win_ref[...], seq_scr[...])
    stage_a[3 * width : 4 * width, :] = dot_tn(wout_ref[...], cot_ref[...])
    for s in range(4):
        for c in range(2):
            stage_b[pl.ds(2 * s + c, count, stride=8), :] = stage_a[
                pl.ds(width * s + c, count, stride=2), :
            ]
    send1[...] = stage_b[...].reshape(count, 8, lanes).astype(bf16)

    pl.semaphore_wait(barrier, count - 1)
    exchange(lambda peer: send1.at[peer], recv1, 0)

    twr = tw_ref[:, 0:lanes]
    twi = tw_ref[:, lanes : 2 * lanes]
    first = (t1h[...], t1l[...])
    second = (t2h[...], t2l[...])
    second_back = (u2h[...], u2l[...])
    first_back = (u1h[...], u1l[...])

    def forward(signals):
        data = halves(jnp.concatenate(signals, axis=1))
        mid = dot3(first, data)
        rows = []
        for i in range(len(signals)):
            re = mid[0:blocks, i * lanes : (i + 1) * lanes]
            im = mid[blocks : 2 * blocks, i * lanes : (i + 1) * lanes]
            rows.append(
                jnp.concatenate([re * twr - im * twi, re * twi + im * twr], axis=1)
            )
        out = dot3(halves(jnp.concatenate(rows, axis=0)), second)
        return [out[i * blocks : (i + 1) * blocks, :] for i in range(len(signals))]

    def backward(spectra):
        mid = dot3(halves(jnp.concatenate(spectra, axis=0)), second_back)
        columns = []
        for i in range(len(spectra)):
            re = mid[i * blocks : (i + 1) * blocks, 0:lanes]
            im = mid[i * blocks : (i + 1) * blocks, lanes : 2 * lanes]
            columns.append(
                jnp.concatenate([re * twr + im * twi, im * twr - re * twi], axis=0)
            )
        out = dot3(first_back, halves(jnp.concatenate(columns, axis=1)))
        return [out[:, i * lanes : (i + 1) * lanes] for i in range(len(spectra))]

    def times(a, b):
        ar, ai = a[:, 0:lanes], a[:, lanes : 2 * lanes]
        br, bi = b[:, 0:lanes], b[:, lanes : 2 * lanes]
        return jnp.concatenate([ar * br - ai * bi, ar * bi + ai * br], axis=1)

    def conj_times(a, b):
        ar, ai = a[:, 0:lanes], a[:, lanes : 2 * lanes]
        br, bi = b[:, 0:lanes], b[:, lanes : 2 * lanes]
        return jnp.concatenate([ar * br + ai * bi, ar * bi - ai * br], axis=1)

    lane_id = lax.broadcasted_iota(jnp.int32, (blocks, lanes), 1)
    row_id = lax.broadcasted_iota(jnp.int32, (blocks, lanes), 0)

    def earlier(x, steps):
        turned = pltpu.roll(x, steps, 1)
        above = jnp.where(row_id == 0, 0.0, pltpu.roll(turned, 1, 0))
        return jnp.where(lane_id < steps, above, turned)

    def later(x, steps):
        turned = pltpu.roll(x, lanes - steps, 1)
        below = jnp.where(row_id == blocks - 1, 0.0, pltpu.roll(turned, blocks - 1, 0))
        return jnp.where(lane_id >= lanes - steps, below, turned)

    filters = [
        ref[pl.ds(c, count, stride=2), :] for ref in (filt1_ref, filt2_ref) for c in range(2)
    ]
    spec_f = forward(filters)
    spec_f1, spec_f2 = spec_f[0:2], spec_f[2:4]

    arrived(recv1, 0)
    stage_b[...] = recv1[...].astype(f32).reshape(count * 8, lanes)

    def tap(s, c, k):
        return taps_ref[pl.ds(width * s + 2 * me + c, 1), k : k + 1]

    shifted = []
    streams = []
    for s in range(3):
        for c in range(2):
            now = stage_b[pl.ds(2 * s + c, count, stride=8), :]
            moved = [now, earlier(now, 1), earlier(now, 2)]
            mixed = tap(s, c, 0) * now
            for k in range(1, 3):
                mixed = mixed + tap(s, c, k) * moved[k]
            shifted.append(moved)
            streams.append(mixed.astype(bf16).astype(f32))
    value, gate_one, gate_two = streams[0:2], streams[2:4], streams[4:6]
    out_grad = [stage_b[pl.ds(6 + c, count, stride=8), :] for c in range(2)]
    grad_second_mix = [out_grad[c] * gate_two[c] for c in range(2)]

    spec = forward(value + grad_second_mix)
    spec_value, spec_gsm = spec[0:2], spec[2:4]
    mixes = backward(
        [times(spec_f1[c], spec_value[c]) for c in range(2)]
        + [conj_times(spec_f2[c], spec_gsm[c]) for c in range(2)]
    )
    first_mix, grad_first_out = mixes[0:2], mixes[2:4]
    first_out = [gate_one[c] * first_mix[c] for c in range(2)]
    grad_first_mix = [gate_one[c] * grad_first_out[c] for c in range(2)]
    spec = forward(first_out + grad_first_mix)
    spec_fo, spec_gfm = spec[0:2], spec[2:4]
    mixes = backward(
        [times(spec_f2[c], spec_fo[c]) for c in range(2)]
        + [conj_times(spec_f1[c], spec_gfm[c]) for c in range(2)]
    )
    second_mix, grad_value = mixes[0:2], mixes[2:4]
    grad_streams = (
        [g.astype(bf16).astype(f32) for g in grad_value]
        + [(grad_first_out[c] * first_mix[c]).astype(bf16).astype(f32) for c in range(2)]
        + [(out_grad[c] * second_mix[c]).astype(bf16).astype(f32) for c in range(2)]
    )
    for s in range(3):
        for c in range(2):
            g = grad_streams[2 * s + c]
            total = tap(s, c, 0) * g
            for k in range(1, 3):
                total = total + tap(s, c, k) * later(g, k)
            stage_a[pl.ds(2 * s + c, count, stride=8), :] = total
    for c in range(2):
        stage_a[pl.ds(6 + c, count, stride=8), :] = gate_two[c] * second_mix[c]
    send2[...] = stage_a[...].reshape(count, 8, lanes).astype(bf16)
    exchange(lambda peer: send2.at[peer], recv2, 1)

    line = jnp.zeros((1, lanes), f32)
    short_lane = lax.broadcasted_iota(jnp.int32, (1, lanes), 1)
    for j in range(6):
        for k in range(3):
            part = jnp.sum(grad_streams[j] * shifted[j][k], axis=0, keepdims=True)
            part = jnp.sum(part, axis=1, keepdims=True)
            line = jnp.where(short_lane == 3 * j + k, part * scale, line)
    short_slab[...] = line
    exchange(lambda peer: short_slab, recv_short, 2)
    grads = backward(
        [conj_times(spec_value[c], spec_gfm[c]) for c in range(2)]
        + [conj_times(spec_fo[c], spec_gsm[c]) for c in range(2)]
    )
    for c in range(2):
        gf1_ref[pl.ds(c, count, stride=2), :] = grads[c] * scale
        gf2_ref[pl.ds(c, count, stride=2), :] = grads[2 + c] * scale

    arrived(recv2, 1)
    stage_b[...] = recv2[...].astype(f32).reshape(count * 8, lanes)
    rows = stage_b[...].astype(bf16)
    with_seq = dot_nt(rows, seq_scr[...])
    with_cot = dot_nt(rows, cot_ref[...])
    kind = lax.broadcasted_iota(jnp.int32, (count * 8, 256), 0) % 8
    partial = jnp.where(kind < 6, with_seq, with_cot) * scale
    send3[...] = partial.reshape(count, 8, 256).astype(bf16)
    exchange(lambda peer: send3.at[peer], recv3, 3)

    for s in range(3):
        for c in range(2):
            stage_a[pl.ds(width * s + c, count, stride=2), :] = stage_b[
                pl.ds(2 * s + c, count, stride=8), :
            ]
    grad_projected = stage_a[0 : 3 * width, :].astype(bf16)
    grad_seq = dot_tn(win_ref[...], grad_projected).astype(bf16)
    gfeat_ref[...] = dot_nt(grad_seq, pick).astype(bf16)

    arrived(recv3, 3)
    slab[...] = jnp.sum(recv3[...].astype(f32), axis=0).astype(bf16)
    exchange(lambda peer: slab, recv4, 4)
    arrived(recv_short, 2)
    gathered = recv_short[...].reshape(count, lanes)
    for s in range(3):
        for c in range(2):
            j = 2 * s + c
            gshort_ref[pl.ds(width * s + c, count, stride=2), :] = gathered[:, 3 * j : 3 * j + 3]
    arrived(recv4, 4)
    total = recv4[...].astype(f32).reshape(count * 8, 256)
    for h in range(2):
        stage_b[...] = total[:, h * lanes : (h + 1) * lanes]
        for s in range(4):
            for c in range(2):
                stage_a[pl.ds(width * s + c, count, stride=2), :] = stage_b[
                    pl.ds(2 * s + c, count, stride=8), :
                ]
        gwin_ref[:, h * lanes : (h + 1) * lanes] = stage_a[0 : 3 * width, :]
        gwout_ref[h * lanes : (h + 1) * lanes, :] = stage_a[3 * width : 4 * width, :].T

    sent(send1, 0)
    sent(send2, 1)
    sent(recv_short, 2)
    sent(send3, 3)
    sent(recv4, 4)


def local(
    count, fft_size, features, sink_order, cotangent, w_in, short_taps, w_out, filter_one, filter_two
):
    width, lanes = features.shape
    length = filter_one.shape[1]
    tables = [jnp.asarray(t) for t in transform_tables(count, lanes)]

    def by_row(filt):
        return filt.reshape(2, count, lanes).transpose(1, 0, 2).reshape(2 * count, lanes)

    def by_channel(grad):
        return grad.reshape(count, 2, lanes).transpose(1, 0, 2).reshape(2, length)

    vmem = pl.BlockSpec(memory_space=pltpu.VMEM)
    shape = jax.ShapeDtypeStruct
    out = pl.pallas_call(
        functools.partial(kernel, count, fft_size),
        out_shape=(
            shape((width, lanes), bf16),
            shape((3 * width, width), f32),
            shape((width, width), f32),
            shape((3 * width, 3), f32),
            shape((width, lanes), f32),
            shape((width, lanes), f32),
        ),
        in_specs=[vmem] * 17,
        out_specs=(vmem,) * 6,
        scratch_shapes=[
            pltpu.VMEM((8 * count, lanes), f32),
            pltpu.VMEM((8 * count, lanes), f32),
            pltpu.VMEM((width, lanes), bf16),
            pltpu.VMEM((count, 8, lanes), bf16),
            pltpu.VMEM((count, 8, lanes), bf16),
            pltpu.VMEM((count, 8, lanes), bf16),
            pltpu.VMEM((count, 8, lanes), bf16),
            pltpu.VMEM((count, 8, width), bf16),
            pltpu.VMEM((count, 8, width), bf16),
            pltpu.VMEM((8, width), bf16),
            pltpu.VMEM((count, 8, width), bf16),
            pltpu.VMEM((1, lanes), f32),
            pltpu.VMEM((count, 1, lanes), f32),
            pltpu.SemaphoreType.DMA((5,)),
            pltpu.SemaphoreType.DMA((5,)),
        ],
        compiler_params=pltpu.CompilerParams(collective_id=0, has_side_effects=True),
    )(
        features,
        sink_order,
        cotangent,
        w_in,
        short_taps,
        w_out,
        by_row(filter_one),
        by_row(filter_two),
        *tables,
    )
    gfeat, gwin, gwout, gshort, gf1, gf2 = out
    return gfeat, gwin, gwout, gshort, by_channel(gf1), by_channel(gf2)


def solution(mesh):
    count = mesh.shape["seq"] * mesh.shape["fft"]
    both = ("seq", "fft")
    return jax.shard_map(
        functools.partial(local, count, mesh.shape["fft"]),
        mesh=mesh,
        in_specs=(
            P(None, both),
            P(both, None),
            P(None, both),
            P(),
            P(),
            P(),
            P(both, None),
            P(both, None),
        ),
        out_specs=(P(None, both), P(), P(), P(), P(both, None), P(both, None)),
        check_vma=False,
    )
```

```python
import functools
import math

import jax
import jax.numpy as jnp
import ml_dtypes
import numpy as np
from jax import lax
from jax.experimental import pallas as pl
from jax.experimental.pallas import tpu as pltpu
from jax.sharding import PartitionSpec as P

bf16 = jnp.bfloat16
f32 = jnp.float32
LOGICAL = pl.DeviceIdType.LOGICAL
SIDE = 4


def chip_offsets():
    steps = [(a, b, c) for a in range(SIDE) for b in range(SIDE) for c in range(SIDE) if a + b + c]
    return sorted(steps, key=lambda step: -sum(min(d, SIDE - d) for d in step))


def table_halves(table):
    high = table.astype(ml_dtypes.bfloat16)
    low = (table - high.astype(np.float64)).astype(ml_dtypes.bfloat16)
    return high, low


def transform_tables(blocks, lanes):
    length = blocks * lanes
    shift = 0.25
    row = np.arange(blocks, dtype=np.float64)
    lane = np.arange(lanes, dtype=np.float64)
    outer = -2.0 * np.pi * np.outer(row + shift, row) / blocks
    twist = -2.0 * np.pi * np.outer(row + shift, lane) / length
    inner = -2.0 * np.pi * (np.outer(lane, lane) % lanes) / lanes
    first = np.concatenate([np.cos(outer), np.sin(outer)], axis=0)
    second = np.block(
        [[np.cos(inner), np.sin(inner)], [-np.sin(inner), np.cos(inner)]]
    )
    second_back = second.T
    first_back = np.concatenate([np.cos(outer).T, np.sin(outer).T], axis=1) / length
    twiddle = np.concatenate([np.cos(twist), np.sin(twist)], axis=1).astype(np.float32)
    pieces = [np.concatenate(table_halves(first), axis=1)]
    for table in (second, second_back, first_back):
        pieces.extend(table_halves(table))
    return np.concatenate(pieces, axis=0), twiddle


def halves(x):
    high = x.astype(bf16)
    return high, (x - high.astype(f32)).astype(bf16)


def dot(a, b):
    return jnp.dot(a, b, preferred_element_type=f32)


def dot_nt(a, b):
    return lax.dot_general(a, b, (((1,), (1,)), ((), ())), preferred_element_type=f32)


def dot_tn(a, b):
    return lax.dot_general(a, b, (((0,), (0,)), ((), ())), preferred_element_type=f32)


def dot3(left, right):
    return dot(left[0], right[0]) + (dot(left[0], right[1]) + dot(left[1], right[0]))


def kernel(
    count,
    feat_in,
    order_in,
    cot_in,
    win_in,
    wout_in,
    taps_in,
    filt1_in,
    filt2_in,
    tab_in,
    tw_in,
    sums_out,
    short_out,
    gfeat_out,
    gf1_out,
    gf2_out,
    feat_ref,
    order_ref,
    cot_pair,
    win_ref,
    wout_ref,
    taps_ref,
    filt1_ref,
    filt2_ref,
    tab_ref,
    tw_ref,
    gfeat_ref,
    gf1_ref,
    gf2_ref,
    stage_a,
    stage_b,
    seq_pair,
    send1,
    recv1,
    send2,
    recv2,
    other_rows,
    send3,
    recv3,
    slab,
    sums,
    short_slab,
    shorts,
    in_sem,
    out_sem,
    send_sem,
    recv_sem,
):
    blocks = count
    chips = count // 2
    lanes = 128
    width = 2 * count
    scale = 1.0 / math.sqrt(blocks * lanes)

    seq_index = lax.axis_index("seq")
    fft_index = lax.axis_index("fft")
    core = fft_index % 2
    x = (fft_index // 2) % 2 * 2 + seq_index // SIDE
    y = fft_index // SIDE
    z = seq_index % SIDE
    along_x = [(x + d) % SIDE % 2 * 32 + (x + d) % SIDE // 2 for d in range(SIDE)]
    along_y = [(y + d) % SIDE * 2 for d in range(SIDE)]
    along_z = [(z + d) % SIDE * 8 for d in range(SIDE)]
    chip = along_x[0] + along_y[0] + along_z[0]
    me = 2 * chip + core
    sibling = 2 * chip + (1 - core)
    other_chips = [along_x[a] + along_y[b] + along_z[c] for a, b, c in chip_offsets()]

    loads = [
        pltpu.make_async_copy(source, target, in_sem.at[n])
        for n, (source, target) in enumerate(
            (
                (feat_in, feat_ref),
                (order_in, order_ref),
                (cot_in, cot_pair.at[core]),
                (win_in, win_ref),
                (wout_in, wout_ref),
                (taps_in, taps_ref),
                (filt1_in, filt1_ref),
                (filt2_in, filt2_ref),
                (tab_in, tab_ref),
                (tw_in, tw_ref),
            )
        )
    ]
    for load in loads:
        load.start()
    barrier = pltpu.get_barrier_semaphore()
    for peer_chip in other_chips:
        for c in range(2):
            pl.semaphore_signal(
                barrier, inc=1, device_id=2 * peer_chip + c, device_id_type=LOGICAL
            )
    pl.semaphore_signal(barrier, inc=1, device_id=sibling, device_id_type=LOGICAL)

    def send(source, target, phase, peer):
        copy = pltpu.make_async_remote_copy(
            source,
            target,
            send_sem.at[phase],
            recv_sem.at[phase],
            device_id=peer,
            device_id_type=LOGICAL,
        )
        copy.start()
        return copy

    def exchange(source, target, phase):
        for peer_chip in other_chips:
            send(source(peer_chip), target, phase, 2 * peer_chip + core)
        pltpu.make_async_copy(source(chip), target, recv_sem.at[phase]).start()

    def arrived(whole, phase):
        pltpu.make_async_copy(whole, whole, recv_sem.at[phase]).wait()

    def sent(whole, phase):
        part = whole.at[pl.ds(0, whole.shape[0] - 1)]
        pltpu.make_async_copy(part, part, send_sem.at[phase]).wait()

    for n in range(5):
        loads[n].wait()
    order = order_ref[...]
    pick = jnp.where(
        lax.broadcasted_iota(jnp.int32, (lanes, lanes), 0) == order, 1.0, 0.0
    ).astype(bf16)
    seq_input = dot(feat_ref[...], pick).astype(bf16)
    seq_pair[core] = seq_input
    stage_a[0 : 3 * width, :] = dot(win_ref[...], seq_input)
    stage_a[3 * width : 4 * width, :] = dot_tn(wout_ref[...], cot_pair[core])
    for s in range(4):
        for c in range(2):
            stage_b[pl.ds(2 * s + c, count, stride=8), :] = stage_a[
                pl.ds(width * s + c, count, stride=2), :
            ]
    send1[...] = stage_b[...].reshape(count, 8, lanes).astype(bf16)

    pl.semaphore_wait(barrier, count - 1)
    for peer_chip in other_chips:
        for c in range(2):
            peer = 2 * peer_chip + c
            send(send1.at[peer], recv1.at[me], 0, peer)
    send(send1.at[sibling], recv1.at[me], 0, sibling)
    pltpu.make_async_copy(send1.at[me], recv1.at[me], recv_sem.at[0]).start()
    to_sibling = [
        send(seq_pair.at[core], seq_pair.at[core], 5, sibling),
        send(cot_pair.at[core], cot_pair.at[core], 6, sibling),
    ]

    for n in range(5, 10):
        loads[n].wait()
    twr = tw_ref[:, 0:lanes]
    twi = tw_ref[:, lanes : 2 * lanes]
    first = tab_ref[0:256, :]
    second = (tab_ref[256:512, :], tab_ref[512:768, :])
    second_back = (tab_ref[768:1024, :], tab_ref[1024:1280, :])
    first_back = (tab_ref[1280:1408, :], tab_ref[1408:1536, :])

    def forward(signals):
        high, low = halves(jnp.concatenate(signals, axis=1))
        mid = dot(first, jnp.concatenate([high, high], axis=0)) + dot(first[:, 0:lanes], low)
        rows = []
        for i in range(len(signals)):
            re = mid[0:blocks, i * lanes : (i + 1) * lanes]
            im = mid[blocks : 2 * blocks, i * lanes : (i + 1) * lanes]
            rows.append(
                jnp.concatenate([re * twr - im * twi, re * twi + im * twr], axis=1)
            )
        out = dot3(halves(jnp.concatenate(rows, axis=0)), second)
        return [out[i * blocks : (i + 1) * blocks, :] for i in range(len(signals))]

    def backward(spectra):
        mid = dot3(halves(jnp.concatenate(spectra, axis=0)), second_back)
        columns = []
        for i in range(len(spectra)):
            re = mid[i * blocks : (i + 1) * blocks, 0:lanes]
            im = mid[i * blocks : (i + 1) * blocks, lanes : 2 * lanes]
            columns.append(
                jnp.concatenate([re * twr + im * twi, im * twr - re * twi], axis=0)
            )
        out = dot3(first_back, halves(jnp.concatenate(columns, axis=1)))
        return [out[:, i * lanes : (i + 1) * lanes] for i in range(len(spectra))]

    def times(a, b):
        ar, ai = a[:, 0:lanes], a[:, lanes : 2 * lanes]
        br, bi = b[:, 0:lanes], b[:, lanes : 2 * lanes]
        return jnp.concatenate([ar * br - ai * bi, ar * bi + ai * br], axis=1)

    def conj_times(a, b):
        ar, ai = a[:, 0:lanes], a[:, lanes : 2 * lanes]
        br, bi = b[:, 0:lanes], b[:, lanes : 2 * lanes]
        return jnp.concatenate([ar * br + ai * bi, ar * bi - ai * br], axis=1)

    lane_id = lax.broadcasted_iota(jnp.int32, (blocks, lanes), 1)
    row_id = lax.broadcasted_iota(jnp.int32, (blocks, lanes), 0)

    def earlier(x, steps):
        turned = pltpu.roll(x, steps, 1)
        above = jnp.where(row_id == 0, 0.0, pltpu.roll(turned, 1, 0))
        return jnp.where(lane_id < steps, above, turned)

    def later(x, steps):
        turned = pltpu.roll(x, lanes - steps, 1)
        below = jnp.where(row_id == blocks - 1, 0.0, pltpu.roll(turned, blocks - 1, 0))
        return jnp.where(lane_id >= lanes - steps, below, turned)

    filters = [
        ref[pl.ds(c, count, stride=2), :] for ref in (filt1_ref, filt2_ref) for c in range(2)
    ]
    spec_f = forward(filters)
    spec_f1, spec_f2 = spec_f[0:2], spec_f[2:4]

    arrived(recv1, 0)
    stage_b[...] = recv1[...].astype(f32).reshape(count * 8, lanes)

    def tap(s, c, k):
        return taps_ref[k, width * s + 2 * me + c]

    shifted = []
    streams = []
    for s in range(3):
        for c in range(2):
            now = stage_b[pl.ds(2 * s + c, count, stride=8), :]
            moved = [now, earlier(now, 1), earlier(now, 2)]
            mixed = tap(s, c, 0) * now
            for k in range(1, 3):
                mixed = mixed + tap(s, c, k) * moved[k]
            shifted.append(moved)
            streams.append(mixed.astype(bf16).astype(f32))
    value, gate_one, gate_two = streams[0:2], streams[2:4], streams[4:6]
    out_grad = [stage_b[pl.ds(6 + c, count, stride=8), :] for c in range(2)]
    grad_second_mix = [out_grad[c] * gate_two[c] for c in range(2)]

    spec = forward(value + grad_second_mix)
    spec_value, spec_gsm = spec[0:2], spec[2:4]
    mixes = backward(
        [times(spec_f1[c], spec_value[c]) for c in range(2)]
        + [conj_times(spec_f2[c], spec_gsm[c]) for c in range(2)]
    )
    first_mix, grad_first_out = mixes[0:2], mixes[2:4]
    first_out = [gate_one[c] * first_mix[c] for c in range(2)]
    grad_first_mix = [gate_one[c] * grad_first_out[c] for c in range(2)]
    spec = forward(first_out + grad_first_mix)
    spec_fo, spec_gfm = spec[0:2], spec[2:4]
    mixes = backward(
        [times(spec_f2[c], spec_fo[c]) for c in range(2)]
        + [conj_times(spec_f1[c], spec_gfm[c]) for c in range(2)]
    )
    second_mix, grad_value = mixes[0:2], mixes[2:4]
    grad_streams = (
        [g.astype(bf16).astype(f32) for g in grad_value]
        + [(grad_first_out[c] * first_mix[c]).astype(bf16).astype(f32) for c in range(2)]
        + [(out_grad[c] * second_mix[c]).astype(bf16).astype(f32) for c in range(2)]
    )
    for s in range(3):
        for c in range(2):
            g = grad_streams[2 * s + c]
            total = tap(s, c, 0) * g
            for k in range(1, 3):
                total = total + tap(s, c, k) * later(g, k)
            stage_a[pl.ds(2 * s + c, count, stride=8), :] = total
    for c in range(2):
        stage_a[pl.ds(6 + c, count, stride=8), :] = gate_two[c] * second_mix[c]
    send2[...] = stage_a[...].reshape(chips, 2, 8, lanes).astype(bf16)
    exchange(lambda peer_chip: send2.at[peer_chip], recv2.at[chip], 1)

    line = jnp.zeros((1, lanes), f32)
    short_lane = lax.broadcasted_iota(jnp.int32, (1, lanes), 1)
    for j in range(6):
        for k in range(3):
            part = jnp.sum(grad_streams[j] * shifted[j][k], axis=0, keepdims=True)
            part = jnp.sum(part, axis=1, keepdims=True)
            line = jnp.where(short_lane == 3 * j + k, part * scale, line)
    short_slab[...] = line
    exchange(lambda peer_chip: short_slab, shorts.at[core, chip], 2)
    grads = backward(
        [conj_times(spec_value[c], spec_gfm[c]) for c in range(2)]
        + [conj_times(spec_fo[c], spec_gsm[c]) for c in range(2)]
    )
    for c in range(2):
        gf1_ref[pl.ds(c, count, stride=2), :] = grads[c] * scale
        gf2_ref[pl.ds(c, count, stride=2), :] = grads[2 + c] * scale
    stores = [
        pltpu.make_async_copy(gf1_ref, gf1_out, out_sem.at[0]),
        pltpu.make_async_copy(gf2_ref, gf2_out, out_sem.at[1]),
    ]
    for store in stores:
        store.start()
    for copy in to_sibling:
        copy.wait()
    seq_both = jnp.concatenate([seq_pair[0], seq_pair[1]], axis=1)
    cot_both = jnp.concatenate([cot_pair[0], cot_pair[1]], axis=1)

    arrived(recv2, 1)
    rows_to_sibling = send(recv2.at[:, 1 - core], other_rows, 7, sibling)
    block_rows = [recv2[:, k].astype(f32).reshape(chips * 8, lanes) for k in range(2)]
    rows = jnp.concatenate([r.astype(bf16) for r in block_rows], axis=1)
    with_seq = dot_nt(rows, seq_both)
    with_cot = dot_nt(rows, cot_both)
    kind = lax.broadcasted_iota(jnp.int32, (chips * 8, 256), 0) % 8
    partial = jnp.where(kind < 6, with_seq, with_cot) * scale
    send3[...] = partial.reshape(chips, 8, 256).astype(bf16)
    exchange(lambda peer_chip: send3.at[peer_chip], recv3.at[chip], 3)

    rows_to_sibling.wait()
    own = jnp.where(core == 0, block_rows[0], block_rows[1])
    other = other_rows[...].astype(f32).reshape(chips * 8, lanes)
    stage_b[0 : chips * 8, :] = jnp.where(core == 0, own, other)
    stage_b[chips * 8 : count * 8, :] = jnp.where(core == 0, other, own)
    for half in range(2):
        for s in range(3):
            for c in range(2):
                stage_a[pl.ds(width * s + 2 * half + c, chips, stride=4), :] = stage_b[
                    pl.ds(chips * 8 * half + 2 * s + c, chips, stride=8), :
                ]
    grad_projected = stage_a[0 : 3 * width, :].astype(bf16)
    grad_seq = dot_tn(win_ref[...], grad_projected).astype(bf16)
    gfeat_ref[...] = dot_nt(grad_seq, pick).astype(bf16)
    stores.append(pltpu.make_async_copy(gfeat_ref, gfeat_out, out_sem.at[2]))
    stores[2].start()
    arrived(shorts.at[core], 2)
    shorts_to_sibling = send(shorts.at[core], shorts.at[core], 9, sibling)

    arrived(recv3, 3)
    slab[...] = jnp.sum(recv3[...].astype(f32), axis=0).astype(bf16)
    exchange(lambda peer_chip: slab, sums.at[core, chip], 4)
    shorts_to_sibling.wait()
    stores.append(pltpu.make_async_copy(shorts, short_out, out_sem.at[3]))
    stores[3].start()
    sent(send1, 0)
    sent(send2, 1)
    sent(shorts.at[0], 2)
    sent(send3, 3)
    arrived(sums.at[core], 4)
    sums_to_sibling = send(sums.at[core], sums.at[core], 8, sibling)
    sums_to_sibling.wait()
    sent(sums.at[0], 4)
    stores.append(pltpu.make_async_copy(sums, sums_out, out_sem.at[4]))
    stores[4].start()
    for store in stores:
        store.wait()


def finish_kernel(
    count,
    sums_ref,
    short_ref,
    gfeat_in,
    gf1_in,
    gf2_in,
    gfeat_ref,
    gwin_ref,
    gwout_ref,
    gshort_ref,
    gf1_ref,
    gf2_ref,
    stage_a,
    stage_b,
):
    chips = count // 2
    lanes = 128
    width = 2 * count
    gfeat_ref[...] = gfeat_in[...]
    gf1_ref[...] = gf1_in[...]
    gf2_ref[...] = gf2_in[...]
    for half in range(2):
        stage_a[pl.ds(half, chips, stride=2), :] = short_ref[half].reshape(chips, lanes)
    by_owner = stage_a[0:count, :]
    owner = lax.broadcasted_iota(jnp.int32, (count, width), 0)
    column = lax.broadcasted_iota(jnp.int32, (count, width), 1)
    spread = [
        lax.dot_general(
            by_owner,
            jnp.where(column == 2 * owner + c, 1.0, 0.0),
            (((0,), (0,)), ((), ())),
            preferred_element_type=f32,
            precision=lax.Precision.HIGHEST,
        )
        for c in range(2)
    ]
    for s in range(3):
        gshort_ref[:, width * s : width * (s + 1)] = (
            spread[0][6 * s : 6 * s + 3, :] + spread[1][6 * s + 3 : 6 * s + 6, :]
        )
    total = sums_ref[...].astype(f32).reshape(count * 8, 256)
    for h in range(2):
        stage_b[...] = total[:, h * lanes : (h + 1) * lanes]
        for half in range(2):
            for s in range(4):
                for c in range(2):
                    stage_a[pl.ds(width * s + 2 * half + c, chips, stride=4), :] = stage_b[
                        pl.ds(chips * 8 * half + 2 * s + c, chips, stride=8), :
                    ]
        gwin_ref[:, h * lanes : (h + 1) * lanes] = stage_a[0 : 3 * width, :]
        gwout_ref[h * lanes : (h + 1) * lanes, :] = stage_a[3 * width : 4 * width, :].T


def local(
    count, features, sink_order, cotangent, w_in, short_taps, w_out, filter_one, filter_two
):
    width, lanes = features.shape
    length = filter_one.shape[1]
    chips = count // 2
    tables, twiddle = (jnp.asarray(t) for t in transform_tables(count, lanes))

    def by_row(filt):
        return filt.reshape(2, count, lanes).transpose(1, 0, 2).reshape(2 * count, lanes)

    def by_channel(grad):
        return grad.reshape(count, 2, lanes).transpose(1, 0, 2).reshape(2, length)

    anywhere = pl.BlockSpec(memory_space=pl.ANY)
    vmem = pl.BlockSpec(memory_space=pltpu.VMEM)
    shape = jax.ShapeDtypeStruct
    grad_shapes = (
        shape((width, lanes), bf16),
        shape((width, lanes), f32),
        shape((width, lanes), f32),
    )
    sums, shorts, gfeat, gf1, gf2 = pl.pallas_call(
        functools.partial(kernel, count),
        out_shape=(
            shape((2, chips, 8, width), bf16),
            shape((2, chips, 1, lanes), f32),
            *grad_shapes,
        ),
        in_specs=[anywhere] * 10,
        out_specs=(anywhere,) * 5,
        scratch_shapes=[
            pltpu.VMEM((width, lanes), bf16),
            pltpu.VMEM((1, lanes), jnp.int32),
            pltpu.VMEM((2, width, lanes), bf16),
            pltpu.VMEM((3 * width, width), bf16),
            pltpu.VMEM((width, width), bf16),
            pltpu.SMEM((3, 3 * width), f32),
            pltpu.VMEM((width, lanes), f32),
            pltpu.VMEM((width, lanes), f32),
            pltpu.VMEM(tables.shape, bf16),
            pltpu.VMEM(twiddle.shape, f32),
            pltpu.VMEM((width, lanes), bf16),
            pltpu.VMEM((width, lanes), f32),
            pltpu.VMEM((width, lanes), f32),
            pltpu.VMEM((8 * count, lanes), f32),
            pltpu.VMEM((8 * count, lanes), f32),
            pltpu.VMEM((2, width, lanes), bf16),
            pltpu.VMEM((count, 8, lanes), bf16),
            pltpu.VMEM((count, 8, lanes), bf16),
            pltpu.VMEM((chips, 2, 8, lanes), bf16),
            pltpu.VMEM((chips, 2, 8, lanes), bf16),
            pltpu.VMEM((chips, 8, lanes), bf16),
            pltpu.VMEM((chips, 8, width), bf16),
            pltpu.VMEM((chips, 8, width), bf16),
            pltpu.VMEM((8, width), bf16),
            pltpu.VMEM((2, chips, 8, width), bf16),
            pltpu.VMEM((1, lanes), f32),
            pltpu.VMEM((2, chips, 1, lanes), f32),
            pltpu.SemaphoreType.DMA((10,)),
            pltpu.SemaphoreType.DMA((5,)),
            pltpu.SemaphoreType.DMA((10,)),
            pltpu.SemaphoreType.DMA((10,)),
        ],
        compiler_params=pltpu.CompilerParams(collective_id=0, has_side_effects=True),
        name="hyena_backward",
    )(
        features,
        sink_order,
        cotangent,
        w_in,
        w_out,
        short_taps.T,
        by_row(filter_one),
        by_row(filter_two),
        tables,
        twiddle,
    )
    gfeat, gwin, gwout, gshort, gf1, gf2 = pl.pallas_call(
        functools.partial(finish_kernel, count),
        out_shape=(
            grad_shapes[0],
            shape((3 * width, width), f32),
            shape((width, width), f32),
            shape((3, 3 * width), f32),
            *grad_shapes[1:],
        ),
        in_specs=[vmem] * 5,
        out_specs=(vmem,) * 6,
        scratch_shapes=[
            pltpu.VMEM((8 * count, lanes), f32),
            pltpu.VMEM((8 * count, lanes), f32),
        ],
        name="row_order",
    )(sums, shorts, gfeat, gf1, gf2)
    return gfeat, gwin, gwout, gshort.T, by_channel(gf1), by_channel(gf2)


def solution(mesh):
    count = mesh.shape["seq"] * mesh.shape["fft"]
    both = ("seq", "fft")
    return jax.shard_map(
        functools.partial(local, count),
        mesh=mesh,
        in_specs=(
            P(None, both),
            P(both, None),
            P(None, both),
            P(),
            P(),
            P(),
            P(both, None),
            P(both, None),
        ),
        out_specs=(P(None, both), P(), P(), P(), P(both, None), P(both, None)),
        check_vma=False,
    )
```

```python
import functools
import math

import jax
import jax.numpy as jnp
import ml_dtypes
import numpy as np
from jax import lax
from jax.experimental import pallas as pl
from jax.experimental.pallas import tpu as pltpu
from jax.sharding import PartitionSpec as P

bf16 = jnp.bfloat16
f32 = jnp.float32
LOGICAL = pl.DeviceIdType.LOGICAL
SIDE = 4
FAR = 5


def hops(step):
    return sum(min(d, SIDE - d) for d in step)


def chip_offsets():
    steps = [(a, b, c) for a in range(SIDE) for b in range(SIDE) for c in range(SIDE) if a + b + c]
    return sorted(steps, key=lambda step: -hops(step))


def plane_offsets():
    return [step for step in chip_offsets() if step[0] == 0]


def table_halves(table):
    high = table.astype(ml_dtypes.bfloat16)
    low = (table - high.astype(np.float64)).astype(ml_dtypes.bfloat16)
    return high, low


def transform_tables(blocks, lanes):
    length = blocks * lanes
    shift = 0.25
    row = np.arange(blocks, dtype=np.float64)
    lane = np.arange(lanes, dtype=np.float64)
    outer = -2.0 * np.pi * np.outer(row + shift, row) / blocks
    twist = -2.0 * np.pi * np.outer(row + shift, lane) / length
    inner = -2.0 * np.pi * (np.outer(lane, lane) % lanes) / lanes
    first = np.concatenate([np.cos(outer), np.sin(outer)], axis=0)
    second = np.block(
        [[np.cos(inner), np.sin(inner)], [-np.sin(inner), np.cos(inner)]]
    )
    second_back = second.T
    first_back = np.concatenate([np.cos(outer).T, np.sin(outer).T], axis=1) / length
    twiddle = np.concatenate([np.cos(twist), np.sin(twist)], axis=1).astype(np.float32)
    pieces = [np.concatenate(table_halves(first), axis=1)]
    for table in (second, second_back, first_back):
        pieces.extend(table_halves(table))
    return np.concatenate(pieces, axis=0), twiddle


def halves(x):
    high = x.astype(bf16)
    return high, (x - high.astype(f32)).astype(bf16)


def dot(a, b):
    return jnp.dot(a, b, preferred_element_type=f32)


def dot_nt(a, b):
    return lax.dot_general(a, b, (((1,), (1,)), ((), ())), preferred_element_type=f32)


def dot_tn(a, b):
    return lax.dot_general(a, b, (((0,), (0,)), ((), ())), preferred_element_type=f32)


def dot3(left, right):
    return dot(left[0], right[0]) + (dot(left[0], right[1]) + dot(left[1], right[0]))


def kernel(
    count,
    feat_in,
    order_in,
    cot_in,
    win_in,
    wout_in,
    taps_in,
    filt1_in,
    filt2_in,
    tab_in,
    tw_in,
    sums_out,
    short_out,
    gfeat_out,
    gf1_out,
    gf2_out,
    feat_ref,
    order_ref,
    cot_line,
    win_ref,
    wout_ref,
    taps_ref,
    filt1_ref,
    filt2_ref,
    tab_ref,
    tw_ref,
    gfeat_ref,
    gf1_ref,
    gf2_ref,
    stage_a,
    stage_b,
    seq_line,
    send1,
    recv1,
    send2,
    recv2,
    rows_line,
    send3,
    recv3,
    slab,
    sums,
    short_slab,
    shorts,
    in_sem,
    out_sem,
    send_sem,
    recv_sem,
    ready_sem,
):
    blocks = count
    chips = count // 2
    lanes = 128
    width = 2 * count
    scale = 1.0 / math.sqrt(blocks * lanes)

    seq_index = lax.axis_index("seq")
    fft_index = lax.axis_index("fft")
    core = fft_index % 2
    x = (fft_index // 2) % 2 * 2 + seq_index // SIDE
    y = fft_index // SIDE
    z = seq_index % SIDE
    along_x = [(x + d) % SIDE % 2 * 32 + (x + d) % SIDE // 2 for d in range(SIDE)]
    along_y = [(y + d) % SIDE * 2 for d in range(SIDE)]
    along_z = [(z + d) % SIDE * 8 for d in range(SIDE)]
    chip = along_x[0] + along_y[0] + along_z[0]
    me = 2 * chip + core
    sibling = 2 * chip + (1 - core)
    other_chips = [along_x[a] + along_y[b] + along_z[c] for a, b, c in chip_offsets()]
    in_line = [(x + d) % SIDE % 2 * 2 + (x + d) % SIDE // 2 for d in range(SIDE)]
    line_chips = [along_x[d] + along_y[0] + along_z[0] for d in range(SIDE)]
    here = z * SIDE + y
    plane = [
        ((z + c) % SIDE * SIDE + (y + b) % SIDE, along_x[0] + along_y[b] + along_z[c])
        for _, b, c in plane_offsets()
    ]
    mine = in_line[0]

    loads = [
        pltpu.make_async_copy(source, target, in_sem.at[n])
        for n, (source, target) in enumerate(
            (
                (feat_in, feat_ref),
                (order_in, order_ref),
                (cot_in, cot_line.at[core, mine]),
                (win_in, win_ref),
                (wout_in, wout_ref),
                (taps_in, taps_ref),
                (filt1_in, filt1_ref),
                (filt2_in, filt2_ref),
                (tab_in, tab_ref),
                (tw_in, tw_ref),
            )
        )
    ]
    for load in loads:
        load.start()
    barrier = pltpu.get_barrier_semaphore()
    for peer_chip in other_chips:
        pl.semaphore_signal(
            barrier, inc=1, device_id=2 * peer_chip + core, device_id_type=LOGICAL
        )
    pl.semaphore_signal(barrier, inc=1, device_id=sibling, device_id_type=LOGICAL)

    def send(source, target, phase, peer):
        copy = pltpu.make_async_remote_copy(
            source,
            target,
            send_sem.at[phase],
            recv_sem.at[phase],
            device_id=peer,
            device_id_type=LOGICAL,
        )
        copy.start()
        return copy

    def exchange(source, target, phase):
        for peer_chip in other_chips:
            send(source(peer_chip), target, phase, 2 * peer_chip + core)
        pltpu.make_async_copy(source(chip), target, recv_sem.at[phase]).start()

    def arrived(whole, phase):
        pltpu.make_async_copy(whole, whole, recv_sem.at[phase]).wait()

    def plane_exchange(source, target, phase):
        for place, peer_chip in plane:
            send(source.at[place], target.at[here], phase, 2 * peer_chip + core)
        pltpu.make_async_copy(source.at[here], target.at[here], recv_sem.at[phase]).start()

    def sent(part, phase):
        pltpu.make_async_copy(part, part, send_sem.at[phase]).wait()

    for n in range(5):
        loads[n].wait()
    order = order_ref[...]
    pick = jnp.where(
        lax.broadcasted_iota(jnp.int32, (lanes, lanes), 0) == order, 1.0, 0.0
    ).astype(bf16)
    seq_input = dot(feat_ref[...], pick).astype(bf16)
    seq_line[core, mine] = seq_input
    stage_a[0 : 3 * width, :] = dot(win_ref[...], seq_input)
    stage_a[3 * width : 4 * width, :] = dot_tn(wout_ref[...], cot_line[core, mine])
    for s in range(4):
        for c in range(2):
            stage_b[pl.ds(2 * s + c, count, stride=8), :] = stage_a[
                pl.ds(width * s + c, count, stride=2), :
            ]
    send1[...] = stage_b[...].reshape(count, 8, lanes).astype(bf16)

    pl.semaphore_wait(barrier, chips)
    pl.semaphore_signal(ready_sem, inc=1, device_id=sibling, device_id_type=LOGICAL)
    pl.semaphore_wait(ready_sem, 1)
    for peer_chip in other_chips:
        for c in range(2):
            peer = 2 * peer_chip + c
            send(send1.at[peer], recv1.at[me], 0, peer)
    send(send1.at[sibling], recv1.at[me], 0, sibling)
    pltpu.make_async_copy(send1.at[me], recv1.at[me], recv_sem.at[0]).start()

    for n in range(5, 10):
        loads[n].wait()
    twr = tw_ref[:, 0:lanes]
    twi = tw_ref[:, lanes : 2 * lanes]
    first = tab_ref[0:256, :]
    second = (tab_ref[256:512, :], tab_ref[512:768, :])
    second_back = (tab_ref[768:1024, :], tab_ref[1024:1280, :])
    first_back = (tab_ref[1280:1408, :], tab_ref[1408:1536, :])

    def forward(signals):
        high, low = halves(jnp.concatenate(signals, axis=1))
        mid = dot(first, jnp.concatenate([high, high], axis=0)) + dot(first[:, 0:lanes], low)
        rows = []
        for i in range(len(signals)):
            re = mid[0:blocks, i * lanes : (i + 1) * lanes]
            im = mid[blocks : 2 * blocks, i * lanes : (i + 1) * lanes]
            rows.append(
                jnp.concatenate([re * twr - im * twi, re * twi + im * twr], axis=1)
            )
        out = dot3(halves(jnp.concatenate(rows, axis=0)), second)
        return [out[i * blocks : (i + 1) * blocks, :] for i in range(len(signals))]

    def backward(spectra):
        mid = dot3(halves(jnp.concatenate(spectra, axis=0)), second_back)
        columns = []
        for i in range(len(spectra)):
            re = mid[i * blocks : (i + 1) * blocks, 0:lanes]
            im = mid[i * blocks : (i + 1) * blocks, lanes : 2 * lanes]
            columns.append(
                jnp.concatenate([re * twr + im * twi, im * twr - re * twi], axis=0)
            )
        out = dot3(first_back, halves(jnp.concatenate(columns, axis=1)))
        return [out[:, i * lanes : (i + 1) * lanes] for i in range(len(spectra))]

    def times(a, b):
        ar, ai = a[:, 0:lanes], a[:, lanes : 2 * lanes]
        br, bi = b[:, 0:lanes], b[:, lanes : 2 * lanes]
        return jnp.concatenate([ar * br - ai * bi, ar * bi + ai * br], axis=1)

    def conj_times(a, b):
        ar, ai = a[:, 0:lanes], a[:, lanes : 2 * lanes]
        br, bi = b[:, 0:lanes], b[:, lanes : 2 * lanes]
        return jnp.concatenate([ar * br + ai * bi, ar * bi - ai * br], axis=1)

    lane_id = lax.broadcasted_iota(jnp.int32, (blocks, lanes), 1)
    row_id = lax.broadcasted_iota(jnp.int32, (blocks, lanes), 0)

    def earlier(x, steps):
        turned = pltpu.roll(x, steps, 1)
        above = jnp.where(row_id == 0, 0.0, pltpu.roll(turned, 1, 0))
        return jnp.where(lane_id < steps, above, turned)

    def later(x, steps):
        turned = pltpu.roll(x, lanes - steps, 1)
        below = jnp.where(row_id == blocks - 1, 0.0, pltpu.roll(turned, blocks - 1, 0))
        return jnp.where(lane_id >= lanes - steps, below, turned)

    filters = [
        ref[pl.ds(c, count, stride=2), :] for ref in (filt1_ref, filt2_ref) for c in range(2)
    ]
    spec_f = forward(filters)
    spec_f1, spec_f2 = spec_f[0:2], spec_f[2:4]

    for d in (2, 1, 3):
        own_seq, own_cot = seq_line.at[core, mine], cot_line.at[core, mine]
        send(own_seq, own_seq, 5, 2 * line_chips[d] + core)
        send(own_cot, own_cot, 6, 2 * line_chips[d] + core)

    arrived(recv1, 0)
    stage_b[...] = recv1[...].astype(f32).reshape(count * 8, lanes)

    def tap(s, c, k):
        return taps_ref[k, width * s + 2 * me + c]

    shifted = []
    streams = []
    for s in range(3):
        for c in range(2):
            now = stage_b[pl.ds(2 * s + c, count, stride=8), :]
            moved = [now, earlier(now, 1), earlier(now, 2)]
            mixed = tap(s, c, 0) * now
            for k in range(1, 3):
                mixed = mixed + tap(s, c, k) * moved[k]
            shifted.append(moved)
            streams.append(mixed.astype(bf16).astype(f32))
    value, gate_one, gate_two = streams[0:2], streams[2:4], streams[4:6]
    out_grad = [stage_b[pl.ds(6 + c, count, stride=8), :] for c in range(2)]
    grad_second_mix = [out_grad[c] * gate_two[c] for c in range(2)]

    spec = forward(value + grad_second_mix)
    spec_value, spec_gsm = spec[0:2], spec[2:4]
    mixes = backward(
        [times(spec_f1[c], spec_value[c]) for c in range(2)]
        + [conj_times(spec_f2[c], spec_gsm[c]) for c in range(2)]
    )
    first_mix, grad_first_out = mixes[0:2], mixes[2:4]
    first_out = [gate_one[c] * first_mix[c] for c in range(2)]
    grad_first_mix = [gate_one[c] * grad_first_out[c] for c in range(2)]
    spec = forward(first_out + grad_first_mix)
    spec_fo, spec_gfm = spec[0:2], spec[2:4]
    mixes = backward(
        [times(spec_f2[c], spec_fo[c]) for c in range(2)]
        + [conj_times(spec_f1[c], spec_gfm[c]) for c in range(2)]
    )
    second_mix, grad_value = mixes[0:2], mixes[2:4]
    grad_streams = (
        [g.astype(bf16).astype(f32) for g in grad_value]
        + [(grad_first_out[c] * first_mix[c]).astype(bf16).astype(f32) for c in range(2)]
        + [(out_grad[c] * second_mix[c]).astype(bf16).astype(f32) for c in range(2)]
    )
    for s in range(3):
        for c in range(2):
            g = grad_streams[2 * s + c]
            total = tap(s, c, 0) * g
            for k in range(1, 3):
                total = total + tap(s, c, k) * later(g, k)
            stage_a[pl.ds(2 * s + c, count, stride=8), :] = total
    for c in range(2):
        stage_a[pl.ds(6 + c, count, stride=8), :] = gate_two[c] * second_mix[c]
    outgoing = stage_a[...].reshape(2, SIDE * SIDE, 2, 2, 8, lanes)
    for k in range(2):
        for low in range(2):
            for high in range(2):
                send2[:, 4 * k + 2 * low + high] = outgoing[low, :, high, k].astype(bf16)
    plane_exchange(send2, recv2, 1)
    line_rest = pl.ds(0, SIDE - 1)
    arrived(seq_line.at[0, line_rest], 5)
    arrived(cot_line.at[0, line_rest], 6)
    line_to_sibling = [
        send(seq_line.at[core], seq_line.at[core], 11, sibling),
        send(cot_line.at[core], cot_line.at[core], 12, sibling),
    ]

    line = jnp.zeros((1, lanes), f32)
    short_lane = lax.broadcasted_iota(jnp.int32, (1, lanes), 1)
    for j in range(6):
        for k in range(3):
            part = jnp.sum(grad_streams[j] * shifted[j][k], axis=0, keepdims=True)
            part = jnp.sum(part, axis=1, keepdims=True)
            line = jnp.where(short_lane == 3 * j + k, part * scale, line)
    short_slab[...] = line
    exchange(lambda peer_chip: short_slab, shorts.at[core, chip], 2)
    grads = backward(
        [conj_times(spec_value[c], spec_gfm[c]) for c in range(2)]
        + [conj_times(spec_fo[c], spec_gsm[c]) for c in range(2)]
    )
    for c in range(2):
        gf1_ref[pl.ds(c, count, stride=2), :] = grads[c] * scale
        gf2_ref[pl.ds(c, count, stride=2), :] = grads[2 + c] * scale
    stores = [
        pltpu.make_async_copy(gf1_ref, gf1_out, out_sem.at[0]),
        pltpu.make_async_copy(gf2_ref, gf2_out, out_sem.at[1]),
    ]
    for store in stores:
        store.start()
    for copy in line_to_sibling:
        copy.wait()
    line_blocks = [(k, p) for k in range(2) for p in range(SIDE)]
    seq_all = jnp.concatenate([seq_line[k, p] for k, p in line_blocks], axis=1)
    cot_all = jnp.concatenate([cot_line[k, p] for k, p in line_blocks], axis=1)

    arrived(recv2, 1)
    rows = jnp.concatenate(
        [recv2[:, n].astype(f32).reshape(count, lanes).astype(bf16) for n in range(2 * SIDE)],
        axis=1,
    )
    with_seq = dot_nt(rows, seq_all)
    with_cot = dot_nt(rows, cot_all)
    kind = lax.broadcasted_iota(jnp.int32, (count, 256), 0) % 8
    partial = jnp.where(kind < 6, with_seq, with_cot) * scale
    send3[...] = partial.reshape(SIDE * SIDE, 8, 256).astype(bf16)
    plane_exchange(send3, recv3, 3)
    own_rows = rows_line.at[mine, core]
    for d in (2, 1, 3):
        for c in range(2):
            send(recv2.at[:, SIDE * c + in_line[d]], own_rows, 7, 2 * line_chips[d] + c)
    send(recv2.at[:, SIDE * (1 - core) + mine], own_rows, 7, sibling)
    pltpu.make_async_copy(recv2.at[:, SIDE * core + mine], own_rows, recv_sem.at[7]).start()
    arrived(shorts.at[core], 2)
    shorts_to_sibling = send(shorts.at[core], shorts.at[core], 9, sibling)

    arrived(recv3, 3)
    slab[...] = jnp.sum(recv3[...].astype(f32), axis=0).astype(bf16)
    near = []
    far = 0
    for step, peer_chip in zip(chip_offsets(), other_chips):
        if hops(step) >= FAR:
            for c in range(2):
                send(slab, sums.at[core, chip], 10, 2 * peer_chip + c)
            far += 2
        else:
            send(slab, sums.at[core, chip], 4, 2 * peer_chip + core)
            near.append(peer_chip)
    pltpu.make_async_copy(slab, sums.at[core, chip], recv_sem.at[4]).start()

    arrived(rows_line, 7)
    by_place = [
        jnp.stack([rows_line[k, p].astype(f32) for p in range(2)], axis=1) for k in range(SIDE)
    ]
    stage_b[...] = jnp.stack(
        [jnp.stack([by_place[2 * low + high] for high in range(2)], axis=1) for low in range(2)],
        axis=0,
    ).reshape(count * 8, lanes)
    for s in range(3):
        for c in range(2):
            stage_a[pl.ds(width * s + c, count, stride=2), :] = stage_b[
                pl.ds(2 * s + c, count, stride=8), :
            ]
    grad_projected = stage_a[0 : 3 * width, :].astype(bf16)
    grad_seq = dot_tn(win_ref[...], grad_projected).astype(bf16)
    gfeat_ref[...] = dot_nt(grad_seq, pick).astype(bf16)
    stores.append(pltpu.make_async_copy(gfeat_ref, gfeat_out, out_sem.at[2]))
    stores[2].start()
    shorts_to_sibling.wait()
    stores.append(pltpu.make_async_copy(shorts, short_out, out_sem.at[3]))
    stores[3].start()

    near_slots = sums.at[0, pl.ds(0, len(near) + 1)]
    far_slots = sums.at[0, pl.ds(0, far)]
    arrived(near_slots, 4)
    for peer_chip in near + [chip]:
        send(sums.at[core, peer_chip], sums.at[core, peer_chip], 8, sibling)
    sent(send1.at[pl.ds(0, count - 1)], 0)
    sent(seq_line.at[0, line_rest], 5)
    sent(cot_line.at[0, line_rest], 6)
    sent(shorts.at[0, pl.ds(0, chips - 1)], 2)
    place_rest = pl.ds(0, SIDE * SIDE - 1)
    sent(send2.at[place_rest], 1)
    sent(send3.at[place_rest], 3)
    sent(recv1.at[pl.ds(0, count - SIDE * SIDE)], 7)
    arrived(far_slots, 10)
    arrived(near_slots, 8)
    sent(sums.at[0, pl.ds(0, len(near))], 4)
    sent(far_slots, 10)
    sent(near_slots, 8)
    stores.append(pltpu.make_async_copy(sums, sums_out, out_sem.at[4]))
    stores[4].start()
    for store in stores:
        store.wait()


def finish_kernel(
    count,
    sums_ref,
    short_ref,
    gfeat_in,
    gf1_in,
    gf2_in,
    gfeat_ref,
    gwin_ref,
    gwout_ref,
    gshort_ref,
    gf1_ref,
    gf2_ref,
    stage_a,
    stage_b,
):
    chips = count // 2
    lanes = 128
    width = 2 * count
    gfeat_ref[...] = gfeat_in[...]
    gf1_ref[...] = gf1_in[...]
    gf2_ref[...] = gf2_in[...]
    for half in range(2):
        stage_a[pl.ds(half, chips, stride=2), :] = short_ref[half].reshape(chips, lanes)
    by_owner = stage_a[0:count, :]
    owner = lax.broadcasted_iota(jnp.int32, (count, width), 0)
    column = lax.broadcasted_iota(jnp.int32, (count, width), 1)
    spread = [
        lax.dot_general(
            by_owner,
            jnp.where(column == 2 * owner + c, 1.0, 0.0),
            (((0,), (0,)), ((), ())),
            preferred_element_type=f32,
            precision=lax.Precision.HIGHEST,
        )
        for c in range(2)
    ]
    for s in range(3):
        gshort_ref[:, width * s : width * (s + 1)] = (
            spread[0][6 * s : 6 * s + 3, :] + spread[1][6 * s + 3 : 6 * s + 6, :]
        )
    total = sums_ref[...].astype(f32).reshape(count * 8, 256)
    for h in range(2):
        stage_b[...] = total[:, h * lanes : (h + 1) * lanes]
        for half in range(2):
            for s in range(4):
                for c in range(2):
                    stage_a[pl.ds(width * s + 2 * half + c, chips, stride=4), :] = stage_b[
                        pl.ds(chips * 8 * half + 2 * s + c, chips, stride=8), :
                    ]
        gwin_ref[:, h * lanes : (h + 1) * lanes] = stage_a[0 : 3 * width, :]
        gwout_ref[h * lanes : (h + 1) * lanes, :] = stage_a[3 * width : 4 * width, :].T


def local(
    count, features, sink_order, cotangent, w_in, short_taps, w_out, filter_one, filter_two
):
    width, lanes = features.shape
    length = filter_one.shape[1]
    chips = count // 2
    tables, twiddle = (jnp.asarray(t) for t in transform_tables(count, lanes))

    def by_row(filt):
        return filt.reshape(2, count, lanes).transpose(1, 0, 2).reshape(2 * count, lanes)

    def by_channel(grad):
        return grad.reshape(count, 2, lanes).transpose(1, 0, 2).reshape(2, length)

    anywhere = pl.BlockSpec(memory_space=pl.ANY)
    vmem = pl.BlockSpec(memory_space=pltpu.VMEM)
    shape = jax.ShapeDtypeStruct
    grad_shapes = (
        shape((width, lanes), bf16),
        shape((width, lanes), f32),
        shape((width, lanes), f32),
    )
    sums, shorts, gfeat, gf1, gf2 = pl.pallas_call(
        functools.partial(kernel, count),
        out_shape=(
            shape((2, chips, 8, width), bf16),
            shape((2, chips, 1, lanes), f32),
            *grad_shapes,
        ),
        in_specs=[anywhere] * 10,
        out_specs=(anywhere,) * 5,
        scratch_shapes=[
            pltpu.VMEM((width, lanes), bf16),
            pltpu.VMEM((1, lanes), jnp.int32),
            pltpu.VMEM((2, SIDE, width, lanes), bf16),
            pltpu.VMEM((3 * width, width), bf16),
            pltpu.VMEM((width, width), bf16),
            pltpu.SMEM((3, 3 * width), f32),
            pltpu.VMEM((width, lanes), f32),
            pltpu.VMEM((width, lanes), f32),
            pltpu.VMEM(tables.shape, bf16),
            pltpu.VMEM(twiddle.shape, f32),
            pltpu.VMEM((width, lanes), bf16),
            pltpu.VMEM((width, lanes), f32),
            pltpu.VMEM((width, lanes), f32),
            pltpu.VMEM((8 * count, lanes), f32),
            pltpu.VMEM((8 * count, lanes), f32),
            pltpu.VMEM((2, SIDE, width, lanes), bf16),
            pltpu.VMEM((count, 8, lanes), bf16),
            pltpu.VMEM((count, 8, lanes), bf16),
            pltpu.VMEM((SIDE * SIDE, 2 * SIDE, 8, lanes), bf16),
            pltpu.VMEM((SIDE * SIDE, 2 * SIDE, 8, lanes), bf16),
            pltpu.VMEM((SIDE, 2, SIDE * SIDE, 8, lanes), bf16),
            pltpu.VMEM((SIDE * SIDE, 8, width), bf16),
            pltpu.VMEM((SIDE * SIDE, 8, width), bf16),
            pltpu.VMEM((8, width), bf16),
            pltpu.VMEM((2, chips, 8, width), bf16),
            pltpu.VMEM((1, lanes), f32),
            pltpu.VMEM((2, chips, 1, lanes), f32),
            pltpu.SemaphoreType.DMA((10,)),
            pltpu.SemaphoreType.DMA((5,)),
            pltpu.SemaphoreType.DMA((13,)),
            pltpu.SemaphoreType.DMA((13,)),
            pltpu.SemaphoreType.REGULAR,
        ],
        compiler_params=pltpu.CompilerParams(collective_id=0, has_side_effects=True),
        name="hyena_backward",
    )(
        features,
        sink_order,
        cotangent,
        w_in,
        w_out,
        short_taps.T,
        by_row(filter_one),
        by_row(filter_two),
        tables,
        twiddle,
    )
    gfeat, gwin, gwout, gshort, gf1, gf2 = pl.pallas_call(
        functools.partial(finish_kernel, count),
        out_shape=(
            grad_shapes[0],
            shape((3 * width, width), f32),
            shape((width, width), f32),
            shape((3, 3 * width), f32),
            *grad_shapes[1:],
        ),
        in_specs=[vmem] * 5,
        out_specs=(vmem,) * 6,
        scratch_shapes=[
            pltpu.VMEM((8 * count, lanes), f32),
            pltpu.VMEM((8 * count, lanes), f32),
        ],
        name="row_order",
    )(sums, shorts, gfeat, gf1, gf2)
    return gfeat, gwin, gwout, gshort.T, by_channel(gf1), by_channel(gf2)


def solution(mesh):
    count = mesh.shape["seq"] * mesh.shape["fft"]
    both = ("seq", "fft")
    return jax.shard_map(
        functools.partial(local, count),
        mesh=mesh,
        in_specs=(
            P(None, both),
            P(both, None),
            P(None, both),
            P(),
            P(),
            P(),
            P(both, None),
            P(both, None),
        ),
        out_specs=(P(None, both), P(), P(), P(), P(both, None), P(both, None)),
        check_vma=False,
    )
```

```python
import functools
import math

import jax
import jax.numpy as jnp
import ml_dtypes
import numpy as np
from jax import lax
from jax.experimental import pallas as pl
from jax.experimental.pallas import tpu as pltpu
from jax.sharding import PartitionSpec as P

bf16 = jnp.bfloat16
f32 = jnp.float32
LOGICAL = pl.DeviceIdType.LOGICAL
SIDE = 4
VIA_SIBLING = (3, 4)


def hops(step):
    return sum(min(d, SIDE - d) for d in step)


def chip_offsets():
    steps = [(a, b, c) for a in range(SIDE) for b in range(SIDE) for c in range(SIDE) if a + b + c]
    return sorted(steps, key=lambda step: -hops(step))


def plane_offsets():
    return [step for step in chip_offsets() if step[0] == 0]


def table_halves(table):
    high = table.astype(ml_dtypes.bfloat16)
    low = (table - high.astype(np.float64)).astype(ml_dtypes.bfloat16)
    return high, low


def transform_tables(blocks, lanes):
    length = blocks * lanes
    shift = 0.25
    row = np.arange(blocks, dtype=np.float64)
    lane = np.arange(lanes, dtype=np.float64)
    outer = -2.0 * np.pi * np.outer(row + shift, row) / blocks
    twist = -2.0 * np.pi * np.outer(row + shift, lane) / length
    inner = -2.0 * np.pi * (np.outer(lane, lane) % lanes) / lanes
    first = np.concatenate([np.cos(outer), np.sin(outer)], axis=0)
    second = np.block(
        [[np.cos(inner), np.sin(inner)], [-np.sin(inner), np.cos(inner)]]
    )
    second_back = second.T
    first_back = np.concatenate([np.cos(outer).T, np.sin(outer).T], axis=1) / length
    twiddle = np.concatenate([np.cos(twist), np.sin(twist)], axis=1).astype(np.float32)
    pieces = [np.concatenate(table_halves(first), axis=1)]
    for table in (second, second_back, first_back):
        pieces.extend(table_halves(table))
    return np.concatenate(pieces, axis=0), twiddle


def halves(x):
    high = x.astype(bf16)
    return high, (x - high.astype(f32)).astype(bf16)


def dot(a, b):
    return jnp.dot(a, b, preferred_element_type=f32)


def dot_nt(a, b):
    return lax.dot_general(a, b, (((1,), (1,)), ((), ())), preferred_element_type=f32)


def dot_tn(a, b):
    return lax.dot_general(a, b, (((0,), (0,)), ((), ())), preferred_element_type=f32)


def dot3(left, right):
    return dot(left[0], right[0]) + (dot(left[0], right[1]) + dot(left[1], right[0]))


def kernel(
    count,
    feat_in,
    order_in,
    cot_in,
    win_in,
    wout_in,
    taps_in,
    filt1_in,
    filt2_in,
    tab_in,
    tw_in,
    sums,
    short_out,
    gfeat_out,
    gf1_out,
    gf2_out,
    feat_ref,
    order_ref,
    cot_line,
    win_ref,
    wout_ref,
    taps_ref,
    filt1_ref,
    filt2_ref,
    tab_ref,
    tw_ref,
    gfeat_ref,
    gf1_ref,
    gf2_ref,
    gshort_ref,
    stage_a,
    stage_b,
    seq_line,
    send1,
    recv1,
    send2,
    recv2,
    rows_line,
    send3,
    recv3,
    slab,
    short_slab,
    shorts,
    in_sem,
    out_sem,
    send_sem,
    recv_sem,
    ready_sem,
):
    blocks = count
    chips = count // 2
    lanes = 128
    width = 2 * count
    scale = 1.0 / math.sqrt(blocks * lanes)

    seq_index = lax.axis_index("seq")
    fft_index = lax.axis_index("fft")
    core = fft_index % 2
    x = (fft_index // 2) % 2 * 2 + seq_index // SIDE
    y = fft_index // SIDE
    z = seq_index % SIDE
    along_x = [(x + d) % SIDE % 2 * 32 + (x + d) % SIDE // 2 for d in range(SIDE)]
    along_y = [(y + d) % SIDE * 2 for d in range(SIDE)]
    along_z = [(z + d) % SIDE * 8 for d in range(SIDE)]
    chip = along_x[0] + along_y[0] + along_z[0]
    me = 2 * chip + core
    sibling = 2 * chip + (1 - core)
    other_chips = [along_x[a] + along_y[b] + along_z[c] for a, b, c in chip_offsets()]
    in_line = [(x + d) % SIDE % 2 * 2 + (x + d) % SIDE // 2 for d in range(SIDE)]
    line_chips = [along_x[d] + along_y[0] + along_z[0] for d in range(SIDE)]
    here = z * SIDE + y
    plane = [
        ((z + c) % SIDE * SIDE + (y + b) % SIDE, along_x[0] + along_y[b] + along_z[c])
        for _, b, c in plane_offsets()
    ]
    mine = in_line[0]

    barrier = pltpu.get_barrier_semaphore()
    for peer_chip in other_chips:
        pl.semaphore_signal(
            barrier, inc=1, device_id=2 * peer_chip + core, device_id_type=LOGICAL
        )
    pl.semaphore_signal(barrier, inc=1, device_id=sibling, device_id_type=LOGICAL)
    loads = [
        pltpu.make_async_copy(source, target, in_sem.at[n])
        for n, (source, target) in enumerate(
            (
                (feat_in, feat_ref),
                (order_in, order_ref),
                (cot_in, cot_line.at[core, mine]),
                (win_in, win_ref),
                (wout_in, wout_ref),
                (taps_in, taps_ref),
                (filt1_in, filt1_ref),
                (filt2_in, filt2_ref),
                (tab_in, tab_ref),
                (tw_in, tw_ref),
            )
        )
    ]
    for load in loads:
        load.start()

    def send(source, target, phase, peer):
        copy = pltpu.make_async_remote_copy(
            source,
            target,
            send_sem.at[phase],
            recv_sem.at[phase],
            device_id=peer,
            device_id_type=LOGICAL,
        )
        copy.start()
        return copy

    def exchange(source, target, phase):
        for peer_chip in other_chips:
            send(source(peer_chip), target, phase, 2 * peer_chip + core)
        pltpu.make_async_copy(source(chip), target, recv_sem.at[phase]).start()

    def arrived(whole, phase):
        pltpu.make_async_copy(whole, whole, recv_sem.at[phase]).wait()

    def plane_exchange(source, target, phase):
        for place, peer_chip in plane:
            send(source.at[place], target.at[here], phase, 2 * peer_chip + core)
        pltpu.make_async_copy(source.at[here], target.at[here], recv_sem.at[phase]).start()

    def sent(part, phase):
        pltpu.make_async_copy(part, part, send_sem.at[phase]).wait()

    for n in range(5):
        loads[n].wait()
    order = order_ref[...]
    pick = jnp.where(
        lax.broadcasted_iota(jnp.int32, (lanes, lanes), 0) == order, 1.0, 0.0
    ).astype(bf16)
    seq_input = dot(feat_ref[...], pick).astype(bf16)
    seq_line[core, mine] = seq_input
    stage_a[0 : 3 * width, :] = dot(win_ref[...], seq_input)
    stage_a[3 * width : 4 * width, :] = dot_tn(wout_ref[...], cot_line[core, mine])
    for s in range(4):
        for c in range(2):
            stage_b[pl.ds(2 * s + c, count, stride=8), :] = stage_a[
                pl.ds(width * s + c, count, stride=2), :
            ]
    send1[...] = stage_b[...].reshape(count, 8, lanes).astype(bf16)

    pl.semaphore_wait(barrier, chips)
    pl.semaphore_signal(ready_sem, inc=1, device_id=sibling, device_id_type=LOGICAL)
    pl.semaphore_wait(ready_sem, 1)
    for peer_chip in other_chips:
        for c in range(2):
            peer = 2 * peer_chip + c
            send(send1.at[peer], recv1.at[me], 0, peer)
    send(send1.at[sibling], recv1.at[me], 0, sibling)
    pltpu.make_async_copy(send1.at[me], recv1.at[me], recv_sem.at[0]).start()

    for n in range(5, 10):
        loads[n].wait()
    twr = tw_ref[:, 0:lanes]
    twi = tw_ref[:, lanes : 2 * lanes]
    first = tab_ref[0:256, :]
    second = (tab_ref[256:512, :], tab_ref[512:768, :])
    second_back = (tab_ref[768:1024, :], tab_ref[1024:1280, :])
    first_back = (tab_ref[1280:1408, :], tab_ref[1408:1536, :])

    def forward(signals):
        high, low = halves(jnp.concatenate(signals, axis=1))
        mid = dot(first, jnp.concatenate([high, high], axis=0)) + dot(first[:, 0:lanes], low)
        rows = []
        for i in range(len(signals)):
            re = mid[0:blocks, i * lanes : (i + 1) * lanes]
            im = mid[blocks : 2 * blocks, i * lanes : (i + 1) * lanes]
            rows.append(
                jnp.concatenate([re * twr - im * twi, re * twi + im * twr], axis=1)
            )
        out = dot3(halves(jnp.concatenate(rows, axis=0)), second)
        return [out[i * blocks : (i + 1) * blocks, :] for i in range(len(signals))]

    def backward(spectra):
        mid = dot3(halves(jnp.concatenate(spectra, axis=0)), second_back)
        columns = []
        for i in range(len(spectra)):
            re = mid[i * blocks : (i + 1) * blocks, 0:lanes]
            im = mid[i * blocks : (i + 1) * blocks, lanes : 2 * lanes]
            columns.append(
                jnp.concatenate([re * twr + im * twi, im * twr - re * twi], axis=0)
            )
        out = dot3(first_back, halves(jnp.concatenate(columns, axis=1)))
        return [out[:, i * lanes : (i + 1) * lanes] for i in range(len(spectra))]

    def times(a, b):
        ar, ai = a[:, 0:lanes], a[:, lanes : 2 * lanes]
        br, bi = b[:, 0:lanes], b[:, lanes : 2 * lanes]
        return jnp.concatenate([ar * br - ai * bi, ar * bi + ai * br], axis=1)

    def conj_times(a, b):
        ar, ai = a[:, 0:lanes], a[:, lanes : 2 * lanes]
        br, bi = b[:, 0:lanes], b[:, lanes : 2 * lanes]
        return jnp.concatenate([ar * br + ai * bi, ar * bi - ai * br], axis=1)

    lane_id = lax.broadcasted_iota(jnp.int32, (blocks, lanes), 1)
    row_id = lax.broadcasted_iota(jnp.int32, (blocks, lanes), 0)

    def earlier(x, steps):
        turned = pltpu.roll(x, steps, 1)
        above = jnp.where(row_id == 0, 0.0, pltpu.roll(turned, 1, 0))
        return jnp.where(lane_id < steps, above, turned)

    def later(x, steps):
        turned = pltpu.roll(x, lanes - steps, 1)
        below = jnp.where(row_id == blocks - 1, 0.0, pltpu.roll(turned, blocks - 1, 0))
        return jnp.where(lane_id >= lanes - steps, below, turned)

    filters = [
        ref[pl.ds(c, count, stride=2), :] for ref in (filt1_ref, filt2_ref) for c in range(2)
    ]
    spec_f = forward(filters)
    spec_f1, spec_f2 = spec_f[0:2], spec_f[2:4]

    for d in (2, 1, 3):
        own_seq, own_cot = seq_line.at[core, mine], cot_line.at[core, mine]
        send(own_seq, own_seq, 5, 2 * line_chips[d] + core)
        send(own_cot, own_cot, 6, 2 * line_chips[d] + core)

    arrived(recv1, 0)
    stage_b[...] = recv1[...].astype(f32).reshape(count * 8, lanes)

    def tap(s, c, k):
        return taps_ref[k, width * s + 2 * me + c]

    shifted = []
    streams = []
    for s in range(3):
        for c in range(2):
            now = stage_b[pl.ds(2 * s + c, count, stride=8), :]
            moved = [now, earlier(now, 1), earlier(now, 2)]
            mixed = tap(s, c, 0) * now
            for k in range(1, 3):
                mixed = mixed + tap(s, c, k) * moved[k]
            shifted.append(moved)
            streams.append(mixed.astype(bf16).astype(f32))
    value, gate_one, gate_two = streams[0:2], streams[2:4], streams[4:6]
    out_grad = [stage_b[pl.ds(6 + c, count, stride=8), :] for c in range(2)]
    grad_second_mix = [out_grad[c] * gate_two[c] for c in range(2)]

    spec = forward(value + grad_second_mix)
    spec_value, spec_gsm = spec[0:2], spec[2:4]
    mixes = backward(
        [times(spec_f1[c], spec_value[c]) for c in range(2)]
        + [conj_times(spec_f2[c], spec_gsm[c]) for c in range(2)]
    )
    first_mix, grad_first_out = mixes[0:2], mixes[2:4]
    first_out = [gate_one[c] * first_mix[c] for c in range(2)]
    grad_first_mix = [gate_one[c] * grad_first_out[c] for c in range(2)]
    spec = forward(first_out + grad_first_mix)
    spec_fo, spec_gfm = spec[0:2], spec[2:4]
    mixes = backward(
        [times(spec_f2[c], spec_fo[c]) for c in range(2)]
        + [conj_times(spec_f1[c], spec_gfm[c]) for c in range(2)]
    )
    second_mix, grad_value = mixes[0:2], mixes[2:4]
    grad_streams = (
        [g.astype(bf16).astype(f32) for g in grad_value]
        + [(grad_first_out[c] * first_mix[c]).astype(bf16).astype(f32) for c in range(2)]
        + [(out_grad[c] * second_mix[c]).astype(bf16).astype(f32) for c in range(2)]
    )
    for s in range(3):
        for c in range(2):
            g = grad_streams[2 * s + c]
            total = tap(s, c, 0) * g
            for k in range(1, 3):
                total = total + tap(s, c, k) * later(g, k)
            stage_a[pl.ds(2 * s + c, count, stride=8), :] = total
    for c in range(2):
        stage_a[pl.ds(6 + c, count, stride=8), :] = gate_two[c] * second_mix[c]
    outgoing = stage_a[...].reshape(2, SIDE * SIDE, 2, 2, 8, lanes)
    for k in range(2):
        for low in range(2):
            for high in range(2):
                send2[:, 4 * k + 2 * low + high] = outgoing[low, :, high, k].astype(bf16)
    plane_exchange(send2, recv2, 1)
    line_rest = pl.ds(0, SIDE - 1)
    arrived(seq_line.at[0, line_rest], 5)
    arrived(cot_line.at[0, line_rest], 6)
    line_to_sibling = [
        send(seq_line.at[core], seq_line.at[core], 11, sibling),
        send(cot_line.at[core], cot_line.at[core], 12, sibling),
    ]

    line = jnp.zeros((1, lanes), f32)
    short_lane = lax.broadcasted_iota(jnp.int32, (1, lanes), 1)
    for j in range(6):
        for k in range(3):
            part = jnp.sum(grad_streams[j] * shifted[j][k], axis=0, keepdims=True)
            part = jnp.sum(part, axis=1, keepdims=True)
            line = jnp.where(short_lane == 3 * j + k, part * scale, line)
    short_slab[...] = line
    exchange(lambda peer_chip: short_slab, shorts.at[core, chip], 2)
    grads = backward(
        [conj_times(spec_value[c], spec_gfm[c]) for c in range(2)]
        + [conj_times(spec_fo[c], spec_gsm[c]) for c in range(2)]
    )
    for c in range(2):
        gf1_ref[pl.ds(c, count, stride=2), :] = grads[c] * scale
        gf2_ref[pl.ds(c, count, stride=2), :] = grads[2 + c] * scale
    stores = [
        pltpu.make_async_copy(gf1_ref, gf1_out, out_sem.at[0]),
        pltpu.make_async_copy(gf2_ref, gf2_out, out_sem.at[1]),
    ]
    for store in stores:
        store.start()
    for copy in line_to_sibling:
        copy.wait()
    line_blocks = [(k, p) for k in range(2) for p in range(SIDE)]
    seq_all = jnp.concatenate([seq_line[k, p] for k, p in line_blocks], axis=1)
    cot_all = jnp.concatenate([cot_line[k, p] for k, p in line_blocks], axis=1)

    arrived(recv2, 1)
    rows = jnp.concatenate(
        [recv2[:, n].astype(f32).reshape(count, lanes).astype(bf16) for n in range(2 * SIDE)],
        axis=1,
    )
    with_seq = dot_nt(rows, seq_all)
    with_cot = dot_nt(rows, cot_all)
    kind = lax.broadcasted_iota(jnp.int32, (count, 256), 0) % 8
    partial = jnp.where(kind < 6, with_seq, with_cot) * scale
    send3[...] = partial.reshape(SIDE * SIDE, 8, 256).astype(bf16)
    plane_exchange(send3, recv3, 3)
    own_rows = rows_line.at[mine, core]
    for d in (2, 1, 3):
        for c in range(2):
            send(recv2.at[:, SIDE * c + in_line[d]], own_rows, 7, 2 * line_chips[d] + c)
    send(recv2.at[:, SIDE * (1 - core) + mine], own_rows, 7, sibling)
    pltpu.make_async_copy(recv2.at[:, SIDE * core + mine], own_rows, recv_sem.at[7]).start()
    arrived(shorts.at[core], 2)
    shorts_to_sibling = send(shorts.at[core], shorts.at[core], 9, sibling)

    arrived(recv3, 3)
    slab[...] = jnp.sum(recv3[...].astype(f32), axis=0).astype(bf16)
    steps = sorted(
        zip(chip_offsets(), other_chips), key=lambda item: hops(item[0]) not in VIA_SIBLING
    )
    relayed = []
    direct = 0
    own_sums = sums.at[core, chip]
    for step, peer_chip in steps:
        if hops(step) in VIA_SIBLING:
            send(slab, own_sums, 4, 2 * peer_chip + core)
            relayed.append(peer_chip)
        else:
            for c in range(2):
                send(slab, own_sums, 10, 2 * peer_chip + c)
            direct += 2
    send(slab, own_sums, 10, sibling)
    pltpu.make_async_copy(slab, own_sums, recv_sem.at[10]).start()

    arrived(rows_line, 7)
    by_place = [
        jnp.stack([rows_line[k, p].astype(f32) for p in range(2)], axis=1) for k in range(SIDE)
    ]
    stage_b[...] = jnp.stack(
        [jnp.stack([by_place[2 * low + high] for high in range(2)], axis=1) for low in range(2)],
        axis=0,
    ).reshape(count * 8, lanes)
    for s in range(3):
        for c in range(2):
            stage_a[pl.ds(width * s + c, count, stride=2), :] = stage_b[
                pl.ds(2 * s + c, count, stride=8), :
            ]
    grad_projected = stage_a[0 : 3 * width, :].astype(bf16)
    grad_seq = dot_tn(win_ref[...], grad_projected).astype(bf16)
    gfeat_ref[...] = dot_nt(grad_seq, pick).astype(bf16)
    stores.append(pltpu.make_async_copy(gfeat_ref, gfeat_out, out_sem.at[2]))
    stores[2].start()
    shorts_to_sibling.wait()
    for half in range(2):
        stage_a[pl.ds(half, chips, stride=2), :] = shorts[half].reshape(chips, lanes)
    by_owner = stage_a[0:count, :]
    owner = lax.broadcasted_iota(jnp.int32, (count, width), 0)
    column = lax.broadcasted_iota(jnp.int32, (count, width), 1)
    spread = [
        lax.dot_general(
            by_owner,
            jnp.where(column == 2 * owner + c, 1.0, 0.0),
            (((0,), (0,)), ((), ())),
            preferred_element_type=f32,
            precision=lax.Precision.HIGHEST,
        )
        for c in range(2)
    ]
    for s in range(3):
        gshort_ref[:, width * s : width * (s + 1)] = (
            spread[0][6 * s : 6 * s + 3, :] + spread[1][6 * s + 3 : 6 * s + 6, :]
        )
    stores.append(pltpu.make_async_copy(gshort_ref, short_out, out_sem.at[3]))
    stores[3].start()

    relayed_slots = sums.at[0, pl.ds(0, len(relayed))]
    arrived(relayed_slots, 4)
    for peer_chip in relayed:
        send(sums.at[core, peer_chip], sums.at[core, peer_chip], 8, sibling)
    sent(send1.at[pl.ds(0, count - 1)], 0)
    sent(seq_line.at[0, line_rest], 5)
    sent(cot_line.at[0, line_rest], 6)
    sent(shorts.at[0, pl.ds(0, chips - 1)], 2)
    place_rest = pl.ds(0, SIDE * SIDE - 1)
    sent(send2.at[place_rest], 1)
    sent(send3.at[place_rest], 3)
    sent(recv1.at[pl.ds(0, count - SIDE * SIDE)], 7)
    arrived(sums.at[0, pl.ds(0, direct + 2)], 10)
    arrived(relayed_slots, 8)
    sent(relayed_slots, 4)
    sent(sums.at[0, pl.ds(0, direct + 1)], 10)
    sent(relayed_slots, 8)
    for store in stores:
        store.wait()


def finish_kernel(
    count,
    sums_in,
    short_in,
    gfeat_in,
    gf1_in,
    gf2_in,
    gfeat_out,
    gwin_out,
    gwout_out,
    gshort_out,
    gf1_out,
    gf2_out,
    sums_ref,
    gfeat_ref,
    gf1_ref,
    gf2_ref,
    gwout_ref,
    gshort_ref,
    ordered,
    stage,
    in_sem,
    out_sem,
):
    chips = count // 2
    lanes = 128
    width = 2 * count
    loads = [
        pltpu.make_async_copy(source, target, in_sem.at[n])
        for n, (source, target) in enumerate(
            (
                (sums_in, sums_ref),
                (short_in, gshort_ref),
                (gf1_in, gf1_ref),
                (gf2_in, gf2_ref),
                (gfeat_in, gfeat_ref),
            )
        )
    ]
    for load in loads:
        load.start()
    stores = []

    def store(source, target):
        copy = pltpu.make_async_copy(source, target, out_sem.at[len(stores)])
        copy.start()
        stores.append(copy)

    loads[0].wait()
    for h in range(2):
        part = pl.ds(h * lanes, lanes)
        stage[...] = sums_ref[:, :, :, part].astype(f32).reshape(count * 8, lanes)
        for half in range(2):
            for s in range(4):
                for c in range(2):
                    ordered[h, pl.ds(width * s + 2 * half + c, chips, stride=4), :] = stage[
                        pl.ds(chips * 8 * half + 2 * s + c, chips, stride=8), :
                    ]
        store(ordered.at[h, pl.ds(0, 3 * width)], gwin_out.at[:, part])
        gwout_ref[part, :] = ordered[h, 3 * width : 4 * width, :].T
        store(gwout_ref.at[part], gwout_out.at[part])
    for n, (ref, target) in enumerate(((gf1_ref, gf1_out), (gf2_ref, gf2_out), (gfeat_ref, gfeat_out))):
        loads[2 + n].wait()
        store(ref, target)
    loads[1].wait()
    store(gshort_ref, gshort_out)
    for copy in stores:
        copy.wait()


def local(
    count, features, sink_order, cotangent, w_in, short_taps, w_out, filter_one, filter_two
):
    width, lanes = features.shape
    length = filter_one.shape[1]
    chips = count // 2
    tables, twiddle = (jnp.asarray(t) for t in transform_tables(count, lanes))

    def by_row(filt):
        return filt.reshape(2, count, lanes).transpose(1, 0, 2).reshape(2 * count, lanes)

    def by_channel(grad):
        return grad.reshape(count, 2, lanes).transpose(1, 0, 2).reshape(2, length)

    anywhere = pl.BlockSpec(memory_space=pl.ANY)
    shape = jax.ShapeDtypeStruct
    grad_shapes = (
        shape((width, lanes), bf16),
        shape((width, lanes), f32),
        shape((width, lanes), f32),
    )
    sums, shorts, gfeat, gf1, gf2 = pl.pallas_call(
        functools.partial(kernel, count),
        out_shape=(
            shape((2, chips, 8, width), bf16),
            shape((3, 3 * width), f32),
            *grad_shapes,
        ),
        in_specs=[anywhere] * 10,
        out_specs=(anywhere,) * 5,
        scratch_shapes=[
            pltpu.VMEM((width, lanes), bf16),
            pltpu.VMEM((1, lanes), jnp.int32),
            pltpu.VMEM((2, SIDE, width, lanes), bf16),
            pltpu.VMEM((3 * width, width), bf16),
            pltpu.VMEM((width, width), bf16),
            pltpu.SMEM((3, 3 * width), f32),
            pltpu.VMEM((width, lanes), f32),
            pltpu.VMEM((width, lanes), f32),
            pltpu.VMEM(tables.shape, bf16),
            pltpu.VMEM(twiddle.shape, f32),
            pltpu.VMEM((width, lanes), bf16),
            pltpu.VMEM((width, lanes), f32),
            pltpu.VMEM((width, lanes), f32),
            pltpu.VMEM((3, 3 * width), f32),
            pltpu.VMEM((8 * count, lanes), f32),
            pltpu.VMEM((8 * count, lanes), f32),
            pltpu.VMEM((2, SIDE, width, lanes), bf16),
            pltpu.VMEM((count, 8, lanes), bf16),
            pltpu.VMEM((count, 8, lanes), bf16),
            pltpu.VMEM((SIDE * SIDE, 2 * SIDE, 8, lanes), bf16),
            pltpu.VMEM((SIDE * SIDE, 2 * SIDE, 8, lanes), bf16),
            pltpu.VMEM((SIDE, 2, SIDE * SIDE, 8, lanes), bf16),
            pltpu.VMEM((SIDE * SIDE, 8, width), bf16),
            pltpu.VMEM((SIDE * SIDE, 8, width), bf16),
            pltpu.VMEM((8, width), bf16),
            pltpu.VMEM((1, lanes), f32),
            pltpu.VMEM((2, chips, 1, lanes), f32),
            pltpu.SemaphoreType.DMA((10,)),
            pltpu.SemaphoreType.DMA((5,)),
            pltpu.SemaphoreType.DMA((13,)),
            pltpu.SemaphoreType.DMA((13,)),
            pltpu.SemaphoreType.REGULAR,
        ],
        compiler_params=pltpu.CompilerParams(collective_id=0, has_side_effects=True),
        name="hyena_backward",
    )(
        features,
        sink_order,
        cotangent,
        w_in,
        w_out,
        short_taps.T,
        by_row(filter_one),
        by_row(filter_two),
        tables,
        twiddle,
    )
    gfeat, gwin, gwout, gshort, gf1, gf2 = pl.pallas_call(
        functools.partial(finish_kernel, count),
        out_shape=(
            grad_shapes[0],
            shape((3 * width, width), f32),
            shape((width, width), f32),
            shape((3, 3 * width), f32),
            *grad_shapes[1:],
        ),
        in_specs=[anywhere] * 5,
        out_specs=(anywhere,) * 6,
        scratch_shapes=[
            pltpu.VMEM((2, chips, 8, width), bf16),
            pltpu.VMEM((width, lanes), bf16),
            pltpu.VMEM((width, lanes), f32),
            pltpu.VMEM((width, lanes), f32),
            pltpu.VMEM((width, width), f32),
            pltpu.VMEM((3, 3 * width), f32),
            pltpu.VMEM((2, 8 * count, lanes), f32),
            pltpu.VMEM((8 * count, lanes), f32),
            pltpu.SemaphoreType.DMA((5,)),
            pltpu.SemaphoreType.DMA((8,)),
        ],
        name="row_order",
    )(sums, shorts, gfeat, gf1, gf2)
    return gfeat, gwin, gwout, gshort.T, by_channel(gf1), by_channel(gf2)


def solution(mesh):
    count = mesh.shape["seq"] * mesh.shape["fft"]
    both = ("seq", "fft")
    return jax.shard_map(
        functools.partial(local, count),
        mesh=mesh,
        in_specs=(
            P(None, both),
            P(both, None),
            P(None, both),
            P(),
            P(),
            P(),
            P(both, None),
            P(both, None),
        ),
        out_specs=(P(None, both), P(), P(), P(), P(both, None), P(both, None)),
        check_vma=False,
    )
```

```python
import functools
import math

import jax
import jax.numpy as jnp
import ml_dtypes
import numpy as np
from jax import lax
from jax.experimental import pallas as pl
from jax.experimental.pallas import tpu as pltpu
from jax.sharding import PartitionSpec as P

bf16 = jnp.bfloat16
f32 = jnp.float32
LOGICAL = pl.DeviceIdType.LOGICAL
SIDE = 4
VIA_SIBLING = (3, 4)


def hops(step):
    return sum(min(d, SIDE - d) for d in step)


def chip_offsets():
    steps = [(a, b, c) for a in range(SIDE) for b in range(SIDE) for c in range(SIDE) if a + b + c]
    return sorted(steps, key=lambda step: (-hops(step), tuple(-min(d, SIDE - d) for d in step)))


def plane_offsets():
    return [step for step in chip_offsets() if step[0] == 0]


def table_halves(table):
    high = table.astype(ml_dtypes.bfloat16)
    low = (table - high.astype(np.float64)).astype(ml_dtypes.bfloat16)
    return high, low


def transform_tables(blocks, lanes):
    length = blocks * lanes
    shift = 0.25
    row = np.arange(blocks, dtype=np.float64)
    lane = np.arange(lanes, dtype=np.float64)
    outer = -2.0 * np.pi * np.outer(row + shift, row) / blocks
    twist = -2.0 * np.pi * np.outer(row + shift, lane) / length
    inner = -2.0 * np.pi * (np.outer(lane, lane) % lanes) / lanes
    first = np.concatenate([np.cos(outer), np.sin(outer)], axis=0)
    second = np.block(
        [[np.cos(inner), np.sin(inner)], [-np.sin(inner), np.cos(inner)]]
    )
    second_back = second.T
    first_back = np.concatenate([np.cos(outer).T, np.sin(outer).T], axis=1) / length
    twiddle = np.concatenate([np.cos(twist), np.sin(twist)], axis=1).astype(np.float32)
    pieces = [np.concatenate(table_halves(first), axis=1)]
    for table in (second, second_back, first_back):
        pieces.extend(table_halves(table))
    return np.concatenate(pieces, axis=0), twiddle


def halves(x):
    high = x.astype(bf16)
    return high, (x - high.astype(f32)).astype(bf16)


def dot(a, b):
    return jnp.dot(a, b, preferred_element_type=f32)


def dot_nt(a, b):
    return lax.dot_general(a, b, (((1,), (1,)), ((), ())), preferred_element_type=f32)


def dot_tn(a, b):
    return lax.dot_general(a, b, (((0,), (0,)), ((), ())), preferred_element_type=f32)


def dot3(left, right):
    return dot(left[0], right[0]) + (dot(left[0], right[1]) + dot(left[1], right[0]))


def kernel(
    count,
    feat_in,
    order_in,
    cot_in,
    win_in,
    wout_in,
    taps_in,
    filt1_in,
    filt2_in,
    tab_in,
    tw_in,
    sums,
    short_out,
    gfeat_out,
    gf1_out,
    gf2_out,
    feat_ref,
    order_ref,
    cot_line,
    win_ref,
    wout_ref,
    taps_ref,
    filt1_ref,
    filt2_ref,
    tab_ref,
    tw_ref,
    gfeat_ref,
    gf1_ref,
    gf2_ref,
    gshort_ref,
    stage_a,
    stage_b,
    seq_line,
    send1,
    recv1,
    send2,
    recv2,
    rows_line,
    send3,
    recv3,
    slab,
    short_slab,
    shorts,
    in_sem,
    out_sem,
    send_sem,
    recv_sem,
    ready_sem,
):
    blocks = count
    chips = count // 2
    lanes = 128
    width = 2 * count
    scale = 1.0 / math.sqrt(blocks * lanes)

    seq_index = lax.axis_index("seq")
    fft_index = lax.axis_index("fft")
    core = lax.rem(fft_index, 2)
    x = lax.rem(lax.div(fft_index, 2), 2) * 2 + lax.div(seq_index, SIDE)
    y = lax.div(fft_index, SIDE)
    z = lax.rem(seq_index, SIDE)
    turned_x, turned_y, turned_z = ([lax.rem(p + d, SIDE) for d in range(SIDE)] for p in (x, y, z))
    along_x = [lax.rem(p, 2) * 32 + lax.div(p, 2) for p in turned_x]
    along_y = [p * 2 for p in turned_y]
    along_z = [p * 8 for p in turned_z]
    chip = along_x[0] + along_y[0] + along_z[0]
    me = 2 * chip + core
    sibling = 2 * chip + (1 - core)
    other_chips = [along_x[a] + along_y[b] + along_z[c] for a, b, c in chip_offsets()]
    in_line = [lax.rem(p, 2) * 2 + lax.div(p, 2) for p in turned_x]
    line_chips = [along_x[d] + along_y[0] + along_z[0] for d in range(SIDE)]
    here = z * SIDE + y
    plane = [
        (turned_z[c] * SIDE + turned_y[b], along_x[0] + along_y[b] + along_z[c])
        for _, b, c in plane_offsets()
    ]
    mine = in_line[0]

    barrier = pltpu.get_barrier_semaphore()
    for peer_chip in other_chips:
        pl.semaphore_signal(
            barrier, inc=1, device_id=2 * peer_chip + core, device_id_type=LOGICAL
        )
    pl.semaphore_signal(barrier, inc=1, device_id=sibling, device_id_type=LOGICAL)
    loads = [
        pltpu.make_async_copy(source, target, in_sem.at[n])
        for n, (source, target) in enumerate(
            (
                (feat_in, feat_ref),
                (order_in, order_ref),
                (cot_in, cot_line.at[core, mine]),
                (win_in, win_ref),
                (wout_in, wout_ref),
                (taps_in, taps_ref),
                (filt1_in, filt1_ref),
                (filt2_in, filt2_ref),
                (tab_in, tab_ref),
                (tw_in, tw_ref),
            )
        )
    ]
    for load in loads:
        load.start()

    def send(source, target, phase, peer):
        copy = pltpu.make_async_remote_copy(
            source,
            target,
            send_sem.at[phase],
            recv_sem.at[phase],
            device_id=peer,
            device_id_type=LOGICAL,
        )
        copy.start()
        return copy

    def exchange(source, target, phase):
        for peer_chip in other_chips:
            send(source(peer_chip), target, phase, 2 * peer_chip + core)
        pltpu.make_async_copy(source(chip), target, recv_sem.at[phase]).start()

    def arrived(whole, phase):
        pltpu.make_async_copy(whole, whole, recv_sem.at[phase]).wait()

    def plane_exchange(source, target, phase):
        for place, peer_chip in plane:
            send(source.at[place], target.at[here], phase, 2 * peer_chip + core)
        pltpu.make_async_copy(source.at[here], target.at[here], recv_sem.at[phase]).start()

    def sent(part, phase):
        pltpu.make_async_copy(part, part, send_sem.at[phase]).wait()

    for n in range(5):
        loads[n].wait()
    order = order_ref[...]
    pick = jnp.where(
        lax.broadcasted_iota(jnp.int32, (lanes, lanes), 0) == order, 1.0, 0.0
    ).astype(bf16)
    seq_input = dot(feat_ref[...], pick).astype(bf16)
    seq_line[core, mine] = seq_input
    stage_a[0 : 3 * width, :] = dot(win_ref[...], seq_input)
    stage_a[3 * width : 4 * width, :] = dot_tn(wout_ref[...], cot_line[core, mine])
    for s in range(4):
        for c in range(2):
            stage_b[pl.ds(2 * s + c, count, stride=8), :] = stage_a[
                pl.ds(width * s + c, count, stride=2), :
            ]
    send1[...] = stage_b[...].reshape(count, 8, lanes).astype(bf16)

    pl.semaphore_wait(barrier, chips)
    pl.semaphore_signal(ready_sem, inc=1, device_id=sibling, device_id_type=LOGICAL)
    pl.semaphore_wait(ready_sem, 1)
    for peer_chip in other_chips:
        for c in range(2):
            peer = 2 * peer_chip + c
            send(send1.at[peer], recv1.at[me], 0, peer)
    send(send1.at[sibling], recv1.at[me], 0, sibling)
    pltpu.make_async_copy(send1.at[me], recv1.at[me], recv_sem.at[0]).start()

    for n in range(5, 10):
        loads[n].wait()
    twr = tw_ref[:, 0:lanes]
    twi = tw_ref[:, lanes : 2 * lanes]
    first = tab_ref[0:256, :]
    second = (tab_ref[256:512, :], tab_ref[512:768, :])
    second_back = (tab_ref[768:1024, :], tab_ref[1024:1280, :])
    first_back = (tab_ref[1280:1408, :], tab_ref[1408:1536, :])

    def forward(signals):
        high, low = halves(jnp.concatenate(signals, axis=1))
        mid = dot(first, jnp.concatenate([high, high], axis=0)) + dot(first[:, 0:lanes], low)
        rows = []
        for i in range(len(signals)):
            re = mid[0:blocks, i * lanes : (i + 1) * lanes]
            im = mid[blocks : 2 * blocks, i * lanes : (i + 1) * lanes]
            rows.append(
                jnp.concatenate([re * twr - im * twi, re * twi + im * twr], axis=1)
            )
        out = dot3(halves(jnp.concatenate(rows, axis=0)), second)
        return [out[i * blocks : (i + 1) * blocks, :] for i in range(len(signals))]

    def backward(spectra):
        mid = dot3(halves(jnp.concatenate(spectra, axis=0)), second_back)
        columns = []
        for i in range(len(spectra)):
            re = mid[i * blocks : (i + 1) * blocks, 0:lanes]
            im = mid[i * blocks : (i + 1) * blocks, lanes : 2 * lanes]
            columns.append(
                jnp.concatenate([re * twr + im * twi, im * twr - re * twi], axis=0)
            )
        out = dot3(first_back, halves(jnp.concatenate(columns, axis=1)))
        return [out[:, i * lanes : (i + 1) * lanes] for i in range(len(spectra))]

    def times(a, b):
        ar, ai = a[:, 0:lanes], a[:, lanes : 2 * lanes]
        br, bi = b[:, 0:lanes], b[:, lanes : 2 * lanes]
        return jnp.concatenate([ar * br - ai * bi, ar * bi + ai * br], axis=1)

    def conj_times(a, b):
        ar, ai = a[:, 0:lanes], a[:, lanes : 2 * lanes]
        br, bi = b[:, 0:lanes], b[:, lanes : 2 * lanes]
        return jnp.concatenate([ar * br + ai * bi, ar * bi - ai * br], axis=1)

    lane_id = lax.broadcasted_iota(jnp.int32, (blocks, lanes), 1)
    row_id = lax.broadcasted_iota(jnp.int32, (blocks, lanes), 0)

    def earlier(x, steps):
        turned = pltpu.roll(x, steps, 1)
        above = jnp.where(row_id == 0, 0.0, pltpu.roll(turned, 1, 0))
        return jnp.where(lane_id < steps, above, turned)

    def later(x, steps):
        turned = pltpu.roll(x, lanes - steps, 1)
        below = jnp.where(row_id == blocks - 1, 0.0, pltpu.roll(turned, blocks - 1, 0))
        return jnp.where(lane_id >= lanes - steps, below, turned)

    filters = [
        ref[pl.ds(c, count, stride=2), :] for ref in (filt1_ref, filt2_ref) for c in range(2)
    ]
    spec_f = forward(filters)
    spec_f1, spec_f2 = spec_f[0:2], spec_f[2:4]

    for d in (2, 1, 3):
        own_seq, own_cot = seq_line.at[core, mine], cot_line.at[core, mine]
        send(own_seq, own_seq, 5, 2 * line_chips[d] + core)
        send(own_cot, own_cot, 6, 2 * line_chips[d] + core)

    arrived(recv1, 0)
    stage_b[...] = recv1[...].astype(f32).reshape(count * 8, lanes)

    def tap(s, c, k):
        return taps_ref[k, width * s + 2 * me + c]

    shifted = []
    streams = []
    for s in range(3):
        for c in range(2):
            now = stage_b[pl.ds(2 * s + c, count, stride=8), :]
            moved = [now, earlier(now, 1), earlier(now, 2)]
            mixed = tap(s, c, 0) * now
            for k in range(1, 3):
                mixed = mixed + tap(s, c, k) * moved[k]
            shifted.append(moved)
            streams.append(mixed.astype(bf16).astype(f32))
    value, gate_one, gate_two = streams[0:2], streams[2:4], streams[4:6]
    out_grad = [stage_b[pl.ds(6 + c, count, stride=8), :] for c in range(2)]
    grad_second_mix = [out_grad[c] * gate_two[c] for c in range(2)]

    spec = forward(value + grad_second_mix)
    spec_value, spec_gsm = spec[0:2], spec[2:4]
    mixes = backward(
        [times(spec_f1[c], spec_value[c]) for c in range(2)]
        + [conj_times(spec_f2[c], spec_gsm[c]) for c in range(2)]
    )
    first_mix, grad_first_out = mixes[0:2], mixes[2:4]
    first_out = [gate_one[c] * first_mix[c] for c in range(2)]
    grad_first_mix = [gate_one[c] * grad_first_out[c] for c in range(2)]
    spec = forward(first_out + grad_first_mix)
    spec_fo, spec_gfm = spec[0:2], spec[2:4]
    mixes = backward(
        [times(spec_f2[c], spec_fo[c]) for c in range(2)]
        + [conj_times(spec_f1[c], spec_gfm[c]) for c in range(2)]
    )
    second_mix, grad_value = mixes[0:2], mixes[2:4]
    grad_streams = (
        [g.astype(bf16).astype(f32) for g in grad_value]
        + [(grad_first_out[c] * first_mix[c]).astype(bf16).astype(f32) for c in range(2)]
        + [(out_grad[c] * second_mix[c]).astype(bf16).astype(f32) for c in range(2)]
    )
    for s in range(3):
        for c in range(2):
            g = grad_streams[2 * s + c]
            total = tap(s, c, 0) * g
            for k in range(1, 3):
                total = total + tap(s, c, k) * later(g, k)
            stage_a[pl.ds(2 * s + c, count, stride=8), :] = total
    for c in range(2):
        stage_a[pl.ds(6 + c, count, stride=8), :] = gate_two[c] * second_mix[c]
    outgoing = stage_a[...].reshape(2, SIDE * SIDE, 2, 2, 8, lanes)
    for k in range(2):
        for low in range(2):
            for high in range(2):
                send2[:, 4 * k + 2 * low + high] = outgoing[low, :, high, k].astype(bf16)
    plane_exchange(send2, recv2, 1)
    line_rest = pl.ds(0, SIDE - 1)
    arrived(seq_line.at[0, line_rest], 5)
    arrived(cot_line.at[0, line_rest], 6)
    line_to_sibling = [
        send(seq_line.at[core], seq_line.at[core], 11, sibling),
        send(cot_line.at[core], cot_line.at[core], 12, sibling),
    ]

    line = jnp.zeros((1, lanes), f32)
    short_lane = lax.broadcasted_iota(jnp.int32, (1, lanes), 1)
    for j in range(6):
        for k in range(3):
            part = jnp.sum(grad_streams[j] * shifted[j][k], axis=0, keepdims=True)
            part = jnp.sum(part, axis=1, keepdims=True)
            line = jnp.where(short_lane == 3 * j + k, part * scale, line)
    short_slab[...] = line
    grads = backward(
        [conj_times(spec_value[c], spec_gfm[c]) for c in range(2)]
        + [conj_times(spec_fo[c], spec_gsm[c]) for c in range(2)]
    )
    for c in range(2):
        gf1_ref[pl.ds(c, count, stride=2), :] = grads[c] * scale
        gf2_ref[pl.ds(c, count, stride=2), :] = grads[2 + c] * scale
    stores = [
        pltpu.make_async_copy(gf1_ref, gf1_out, out_sem.at[0]),
        pltpu.make_async_copy(gf2_ref, gf2_out, out_sem.at[1]),
    ]
    for store in stores:
        store.start()
    for copy in line_to_sibling:
        copy.wait()
    line_blocks = [(k, p) for k in range(2) for p in range(SIDE)]
    seq_all = jnp.concatenate([seq_line[k, p] for k, p in line_blocks], axis=1)
    cot_all = jnp.concatenate([cot_line[k, p] for k, p in line_blocks], axis=1)

    arrived(recv2, 1)
    rows = jnp.concatenate(
        [recv2[:, n].astype(f32).reshape(count, lanes).astype(bf16) for n in range(2 * SIDE)],
        axis=1,
    )
    with_seq = dot_nt(rows, seq_all)
    with_cot = dot_nt(rows, cot_all)
    kind = lax.broadcasted_iota(jnp.int32, (count, 256), 0) % 8
    partial = jnp.where(kind < 6, with_seq, with_cot) * scale
    send3[...] = partial.reshape(SIDE * SIDE, 8, 256).astype(bf16)
    plane_exchange(send3, recv3, 3)
    exchange(lambda peer_chip: short_slab, shorts.at[core, chip], 2)
    own_rows = rows_line.at[mine, core]
    for d in (2, 1, 3):
        for c in range(2):
            send(recv2.at[:, SIDE * c + in_line[d]], own_rows, 7, 2 * line_chips[d] + c)
    send(recv2.at[:, SIDE * (1 - core) + mine], own_rows, 7, sibling)
    pltpu.make_async_copy(recv2.at[:, SIDE * core + mine], own_rows, recv_sem.at[7]).start()

    arrived(recv3, 3)
    slab[...] = jnp.sum(recv3[...].astype(f32), axis=0).astype(bf16)
    steps = sorted(
        zip(chip_offsets(), other_chips), key=lambda item: hops(item[0]) not in VIA_SIBLING
    )
    relayed = []
    direct = 0
    own_sums = sums.at[core, chip]
    for step, peer_chip in steps:
        if hops(step) in VIA_SIBLING:
            send(slab, own_sums, 4, 2 * peer_chip + core)
            relayed.append(peer_chip)
        else:
            for c in range(2):
                send(slab, own_sums, 10, 2 * peer_chip + c)
            direct += 2
    send(slab, own_sums, 10, sibling)
    pltpu.make_async_copy(slab, own_sums, recv_sem.at[10]).start()

    arrived(shorts.at[core], 2)
    shorts_to_sibling = send(shorts.at[core], shorts.at[core], 9, sibling)
    arrived(rows_line, 7)
    by_place = [
        jnp.stack([rows_line[k, p].astype(f32) for p in range(2)], axis=1) for k in range(SIDE)
    ]
    stage_b[...] = jnp.stack(
        [jnp.stack([by_place[2 * low + high] for high in range(2)], axis=1) for low in range(2)],
        axis=0,
    ).reshape(count * 8, lanes)
    for s in range(3):
        for c in range(2):
            stage_a[pl.ds(width * s + c, count, stride=2), :] = stage_b[
                pl.ds(2 * s + c, count, stride=8), :
            ]
    grad_projected = stage_a[0 : 3 * width, :].astype(bf16)
    grad_seq = dot_tn(win_ref[...], grad_projected).astype(bf16)
    gfeat_ref[...] = dot_nt(grad_seq, pick).astype(bf16)
    stores.append(pltpu.make_async_copy(gfeat_ref, gfeat_out, out_sem.at[2]))
    stores[2].start()
    shorts_to_sibling.wait()
    for half in range(2):
        stage_a[pl.ds(half, chips, stride=2), :] = shorts[half].reshape(chips, lanes)
    by_owner = stage_a[0:count, :]
    owner = lax.broadcasted_iota(jnp.int32, (count, width), 0)
    column = lax.broadcasted_iota(jnp.int32, (count, width), 1)
    spread = [
        lax.dot_general(
            by_owner,
            jnp.where(column == 2 * owner + c, 1.0, 0.0),
            (((0,), (0,)), ((), ())),
            preferred_element_type=f32,
            precision=lax.Precision.HIGHEST,
        )
        for c in range(2)
    ]
    for s in range(3):
        gshort_ref[:, width * s : width * (s + 1)] = (
            spread[0][6 * s : 6 * s + 3, :] + spread[1][6 * s + 3 : 6 * s + 6, :]
        )
    stores.append(pltpu.make_async_copy(gshort_ref, short_out, out_sem.at[3]))
    stores[3].start()

    relayed_slots = sums.at[0, pl.ds(0, len(relayed))]
    arrived(relayed_slots, 4)
    for peer_chip in relayed:
        send(sums.at[core, peer_chip], sums.at[core, peer_chip], 8, sibling)
    sent(send1.at[pl.ds(0, count - 1)], 0)
    sent(seq_line.at[0, line_rest], 5)
    sent(cot_line.at[0, line_rest], 6)
    sent(shorts.at[0, pl.ds(0, chips - 1)], 2)
    place_rest = pl.ds(0, SIDE * SIDE - 1)
    sent(send2.at[place_rest], 1)
    sent(send3.at[place_rest], 3)
    sent(recv1.at[pl.ds(0, count - SIDE * SIDE)], 7)
    arrived(sums.at[0, pl.ds(0, direct + 2)], 10)
    arrived(relayed_slots, 8)
    sent(relayed_slots, 4)
    sent(sums.at[0, pl.ds(0, direct + 1)], 10)
    sent(relayed_slots, 8)
    for store in stores:
        store.wait()


def finish_kernel(
    count,
    sums_in,
    short_in,
    gfeat_in,
    gf1_in,
    gf2_in,
    gfeat_out,
    gwin_out,
    gwout_out,
    gshort_out,
    gf1_out,
    gf2_out,
    sums_ref,
    gfeat_ref,
    gf1_ref,
    gf2_ref,
    gwout_ref,
    gshort_ref,
    ordered,
    stage,
    in_sem,
    out_sem,
):
    chips = count // 2
    lanes = 128
    width = 2 * count
    loads = [
        pltpu.make_async_copy(source, target, in_sem.at[n])
        for n, (source, target) in enumerate(
            (
                (sums_in, sums_ref),
                (short_in, gshort_ref),
                (gf1_in, gf1_ref),
                (gf2_in, gf2_ref),
                (gfeat_in, gfeat_ref),
            )
        )
    ]
    for load in loads:
        load.start()
    stores = []

    def store(source, target):
        copy = pltpu.make_async_copy(source, target, out_sem.at[len(stores)])
        copy.start()
        stores.append(copy)

    loads[0].wait()
    for h in range(2):
        part = pl.ds(h * lanes, lanes)
        stage[...] = sums_ref[:, :, :, part].astype(f32).reshape(count * 8, lanes)
        for half in range(2):
            for s in range(4):
                for c in range(2):
                    ordered[h, pl.ds(width * s + 2 * half + c, chips, stride=4), :] = stage[
                        pl.ds(chips * 8 * half + 2 * s + c, chips, stride=8), :
                    ]
        store(ordered.at[h, pl.ds(0, 3 * width)], gwin_out.at[:, part])
        gwout_ref[part, :] = ordered[h, 3 * width : 4 * width, :].T
        store(gwout_ref.at[part], gwout_out.at[part])
    for n, (ref, target) in enumerate(((gf1_ref, gf1_out), (gf2_ref, gf2_out), (gfeat_ref, gfeat_out))):
        loads[2 + n].wait()
        store(ref, target)
    loads[1].wait()
    store(gshort_ref, gshort_out)
    for copy in stores:
        copy.wait()


def local(
    count, features, sink_order, cotangent, w_in, short_taps, w_out, filter_one, filter_two
):
    width, lanes = features.shape
    length = filter_one.shape[1]
    chips = count // 2
    tables, twiddle = (jnp.asarray(t) for t in transform_tables(count, lanes))

    def by_row(filt):
        return filt.reshape(2, count, lanes).transpose(1, 0, 2).reshape(2 * count, lanes)

    def by_channel(grad):
        return grad.reshape(count, 2, lanes).transpose(1, 0, 2).reshape(2, length)

    anywhere = pl.BlockSpec(memory_space=pl.ANY)
    shape = jax.ShapeDtypeStruct
    grad_shapes = (
        shape((width, lanes), bf16),
        shape((width, lanes), f32),
        shape((width, lanes), f32),
    )
    sums, shorts, gfeat, gf1, gf2 = pl.pallas_call(
        functools.partial(kernel, count),
        out_shape=(
            shape((2, chips, 8, width), bf16),
            shape((3, 3 * width), f32),
            *grad_shapes,
        ),
        in_specs=[anywhere] * 10,
        out_specs=(anywhere,) * 5,
        scratch_shapes=[
            pltpu.VMEM((width, lanes), bf16),
            pltpu.VMEM((1, lanes), jnp.int32),
            pltpu.VMEM((2, SIDE, width, lanes), bf16),
            pltpu.VMEM((3 * width, width), bf16),
            pltpu.VMEM((width, width), bf16),
            pltpu.SMEM((3, 3 * width), f32),
            pltpu.VMEM((width, lanes), f32),
            pltpu.VMEM((width, lanes), f32),
            pltpu.VMEM(tables.shape, bf16),
            pltpu.VMEM(twiddle.shape, f32),
            pltpu.VMEM((width, lanes), bf16),
            pltpu.VMEM((width, lanes), f32),
            pltpu.VMEM((width, lanes), f32),
            pltpu.VMEM((3, 3 * width), f32),
            pltpu.VMEM((8 * count, lanes), f32),
            pltpu.VMEM((8 * count, lanes), f32),
            pltpu.VMEM((2, SIDE, width, lanes), bf16),
            pltpu.VMEM((count, 8, lanes), bf16),
            pltpu.VMEM((count, 8, lanes), bf16),
            pltpu.VMEM((SIDE * SIDE, 2 * SIDE, 8, lanes), bf16),
            pltpu.VMEM((SIDE * SIDE, 2 * SIDE, 8, lanes), bf16),
            pltpu.VMEM((SIDE, 2, SIDE * SIDE, 8, lanes), bf16),
            pltpu.VMEM((SIDE * SIDE, 8, width), bf16),
            pltpu.VMEM((SIDE * SIDE, 8, width), bf16),
            pltpu.VMEM((8, width), bf16),
            pltpu.VMEM((1, lanes), f32),
            pltpu.VMEM((2, chips, 1, lanes), f32),
            pltpu.SemaphoreType.DMA((10,)),
            pltpu.SemaphoreType.DMA((5,)),
            pltpu.SemaphoreType.DMA((13,)),
            pltpu.SemaphoreType.DMA((13,)),
            pltpu.SemaphoreType.REGULAR,
        ],
        compiler_params=pltpu.CompilerParams(collective_id=0, has_side_effects=True),
        name="hyena_backward",
    )(
        features,
        sink_order,
        cotangent,
        w_in,
        w_out,
        short_taps.T,
        by_row(filter_one),
        by_row(filter_two),
        tables,
        twiddle,
    )
    gfeat, gwin, gwout, gshort, gf1, gf2 = pl.pallas_call(
        functools.partial(finish_kernel, count),
        out_shape=(
            grad_shapes[0],
            shape((3 * width, width), f32),
            shape((width, width), f32),
            shape((3, 3 * width), f32),
            *grad_shapes[1:],
        ),
        in_specs=[anywhere] * 5,
        out_specs=(anywhere,) * 6,
        scratch_shapes=[
            pltpu.VMEM((2, chips, 8, width), bf16),
            pltpu.VMEM((width, lanes), bf16),
            pltpu.VMEM((width, lanes), f32),
            pltpu.VMEM((width, lanes), f32),
            pltpu.VMEM((width, width), f32),
            pltpu.VMEM((3, 3 * width), f32),
            pltpu.VMEM((2, 8 * count, lanes), f32),
            pltpu.VMEM((8 * count, lanes), f32),
            pltpu.SemaphoreType.DMA((5,)),
            pltpu.SemaphoreType.DMA((8,)),
        ],
        name="row_order",
    )(sums, shorts, gfeat, gf1, gf2)
    return gfeat, gwin, gwout, gshort.T, by_channel(gf1), by_channel(gf2)


def solution(mesh):
    count = mesh.shape["seq"] * mesh.shape["fft"]
    both = ("seq", "fft")
    return jax.shard_map(
        functools.partial(local, count),
        mesh=mesh,
        in_specs=(
            P(None, both),
            P(both, None),
            P(None, both),
            P(),
            P(),
            P(),
            P(both, None),
            P(both, None),
        ),
        out_specs=(P(None, both), P(), P(), P(), P(both, None), P(both, None)),
        check_vma=False,
    )
```

```python
import functools
import math

import jax
import jax.numpy as jnp
import ml_dtypes
import numpy as np
from jax import lax
from jax.experimental import pallas as pl
from jax.experimental.pallas import tpu as pltpu
from jax.sharding import PartitionSpec as P

bf16 = jnp.bfloat16
f32 = jnp.float32
LOGICAL = pl.DeviceIdType.LOGICAL
SIDE = 4
VIA_SIBLING = (3, 4)


def hops(step):
    return sum(min(d, SIDE - d) for d in step)


def chip_offsets():
    steps = [(a, b, c) for a in range(SIDE) for b in range(SIDE) for c in range(SIDE) if a + b + c]
    return sorted(steps, key=lambda step: (-hops(step), tuple(-min(d, SIDE - d) for d in step)))


def plane_offsets():
    return [step for step in chip_offsets() if step[0] == 0]


def table_halves(table):
    high = table.astype(ml_dtypes.bfloat16)
    low = (table - high.astype(np.float64)).astype(ml_dtypes.bfloat16)
    return high, low


def transform_tables(blocks, lanes):
    length = blocks * lanes
    shift = 0.25
    row = np.arange(blocks, dtype=np.float64)
    lane = np.arange(lanes, dtype=np.float64)
    outer = -2.0 * np.pi * np.outer(row + shift, row) / blocks
    twist = -2.0 * np.pi * np.outer(row + shift, lane) / length
    inner = -2.0 * np.pi * (np.outer(lane, lane) % lanes) / lanes
    first = np.concatenate([np.cos(outer), np.sin(outer)], axis=0)
    second = np.block(
        [[np.cos(inner), np.sin(inner)], [-np.sin(inner), np.cos(inner)]]
    )
    second_back = second.T
    first_back = np.concatenate([np.cos(outer).T, np.sin(outer).T], axis=1) / length
    twiddle = np.concatenate([np.cos(twist), np.sin(twist)], axis=1).astype(np.float32)
    pieces = [np.concatenate(table_halves(first), axis=1)]
    for table in (second, second_back, first_back):
        pieces.extend(table_halves(table))
    return np.concatenate(pieces, axis=0), twiddle


def halves(x):
    high = x.astype(bf16)
    return high, (x - high.astype(f32)).astype(bf16)


def dot(a, b):
    return jnp.dot(a, b, preferred_element_type=f32)


def dot_nt(a, b):
    return lax.dot_general(a, b, (((1,), (1,)), ((), ())), preferred_element_type=f32)


def dot_tn(a, b):
    return lax.dot_general(a, b, (((0,), (0,)), ((), ())), preferred_element_type=f32)


def dot3(left, right):
    return dot(left[0], right[0]) + (dot(left[0], right[1]) + dot(left[1], right[0]))


def kernel(
    count,
    feat_in,
    order_in,
    cot_in,
    win_in,
    wout_in,
    taps_in,
    filt1_in,
    filt2_in,
    tab_in,
    tw_in,
    sums,
    short_out,
    gfeat_out,
    gf1_out,
    gf2_out,
    feat_ref,
    order_ref,
    cot_line,
    win_ref,
    wout_ref,
    taps_ref,
    filt1_ref,
    filt2_ref,
    tab_ref,
    tw_ref,
    gfeat_ref,
    gf1_ref,
    gf2_ref,
    gshort_ref,
    stage_a,
    stage_b,
    seq_line,
    send1,
    recv1,
    send2,
    recv2,
    rows_line,
    send3,
    recv3,
    slab,
    short_slab,
    shorts,
    in_sem,
    out_sem,
    send_sem,
    recv_sem,
    ready_sem,
):
    blocks = count
    chips = count // 2
    lanes = 128
    width = 2 * count
    scale = 1.0 / math.sqrt(blocks * lanes)

    seq_index = lax.axis_index("seq")
    fft_index = lax.axis_index("fft")
    core = lax.rem(fft_index, 2)
    x = lax.rem(lax.div(fft_index, 2), 2) * 2 + lax.div(seq_index, SIDE)
    y = lax.div(fft_index, SIDE)
    z = lax.rem(seq_index, SIDE)
    turned_x, turned_y, turned_z = ([lax.rem(p + d, SIDE) for d in range(SIDE)] for p in (x, y, z))
    along_x = [lax.rem(p, 2) * 32 + lax.div(p, 2) for p in turned_x]
    along_y = [p * 2 for p in turned_y]
    along_z = [p * 8 for p in turned_z]
    chip = along_x[0] + along_y[0] + along_z[0]
    me = 2 * chip + core
    sibling = 2 * chip + (1 - core)
    other_chips = [along_x[a] + along_y[b] + along_z[c] for a, b, c in chip_offsets()]
    in_line = [lax.rem(p, 2) * 2 + lax.div(p, 2) for p in turned_x]
    line_chips = [along_x[d] + along_y[0] + along_z[0] for d in range(SIDE)]
    here = z * SIDE + y
    plane = [
        (turned_z[c] * SIDE + turned_y[b], along_x[0] + along_y[b] + along_z[c])
        for _, b, c in plane_offsets()
    ]
    mine = in_line[0]

    barrier = pltpu.get_barrier_semaphore()
    for peer_chip in other_chips:
        pl.semaphore_signal(
            barrier, inc=1, device_id=2 * peer_chip + core, device_id_type=LOGICAL
        )
    pl.semaphore_signal(barrier, inc=1, device_id=sibling, device_id_type=LOGICAL)
    loads = [
        pltpu.make_async_copy(source, target, in_sem.at[n])
        for n, (source, target) in enumerate(
            (
                (feat_in, feat_ref),
                (order_in, order_ref),
                (cot_in, cot_line.at[core, mine]),
                (win_in, win_ref),
                (wout_in, wout_ref),
                (taps_in, taps_ref),
                (filt1_in, filt1_ref),
                (filt2_in, filt2_ref),
                (tab_in, tab_ref),
                (tw_in, tw_ref),
            )
        )
    ]
    for load in loads:
        load.start()

    def send(source, target, phase, peer):
        copy = pltpu.make_async_remote_copy(
            source,
            target,
            send_sem.at[phase],
            recv_sem.at[phase],
            device_id=peer,
            device_id_type=LOGICAL,
        )
        copy.start()
        return copy

    def exchange(source, target, phase):
        for peer_chip in other_chips:
            send(source(peer_chip), target, phase, 2 * peer_chip + core)
        pltpu.make_async_copy(source(chip), target, recv_sem.at[phase]).start()

    def arrived(whole, phase):
        pltpu.make_async_copy(whole, whole, recv_sem.at[phase]).wait()

    def plane_exchange(source, target, phase):
        for place, peer_chip in plane:
            send(source.at[place], target.at[here], phase, 2 * peer_chip + core)
        pltpu.make_async_copy(source.at[here], target.at[here], recv_sem.at[phase]).start()

    def sent(part, phase):
        pltpu.make_async_copy(part, part, send_sem.at[phase]).wait()

    for n in range(5):
        loads[n].wait()
    order = order_ref[...]
    pick = jnp.where(
        lax.broadcasted_iota(jnp.int32, (lanes, lanes), 0) == order, 1.0, 0.0
    ).astype(bf16)
    seq_input = dot(feat_ref[...], pick).astype(bf16)
    seq_line[core, mine] = seq_input
    stage_a[0 : 3 * width, :] = dot(win_ref[...], seq_input)
    stage_a[3 * width : 4 * width, :] = dot_tn(wout_ref[...], cot_line[core, mine])
    for s in range(4):
        for c in range(2):
            stage_b[pl.ds(2 * s + c, count, stride=8), :] = stage_a[
                pl.ds(width * s + c, count, stride=2), :
            ]
    send1[...] = stage_b[...].reshape(count, 8, lanes).astype(bf16)

    pl.semaphore_wait(barrier, chips)
    pl.semaphore_signal(ready_sem, inc=1, device_id=sibling, device_id_type=LOGICAL)
    pl.semaphore_wait(ready_sem, 1)
    for peer_chip in other_chips:
        for c in range(2):
            peer = 2 * peer_chip + c
            send(send1.at[peer], recv1.at[me], 0, peer)
    send(send1.at[sibling], recv1.at[me], 0, sibling)
    pltpu.make_async_copy(send1.at[me], recv1.at[me], recv_sem.at[0]).start()

    for n in range(5, 10):
        loads[n].wait()
    twr = tw_ref[:, 0:lanes]
    twi = tw_ref[:, lanes : 2 * lanes]
    first = tab_ref[0:256, :]
    second = (tab_ref[256:512, :], tab_ref[512:768, :])
    second_back = (tab_ref[768:1024, :], tab_ref[1024:1280, :])
    first_back = (tab_ref[1280:1408, :], tab_ref[1408:1536, :])

    def forward(signals):
        high, low = halves(jnp.concatenate(signals, axis=1))
        mid = dot(first, jnp.concatenate([high, high], axis=0)) + dot(first[:, 0:lanes], low)
        rows = []
        for i in range(len(signals)):
            re = mid[0:blocks, i * lanes : (i + 1) * lanes]
            im = mid[blocks : 2 * blocks, i * lanes : (i + 1) * lanes]
            rows.append(
                jnp.concatenate([re * twr - im * twi, re * twi + im * twr], axis=1)
            )
        out = dot3(halves(jnp.concatenate(rows, axis=0)), second)
        return [out[i * blocks : (i + 1) * blocks, :] for i in range(len(signals))]

    def backward(spectra):
        mid = dot3(halves(jnp.concatenate(spectra, axis=0)), second_back)
        columns = []
        for i in range(len(spectra)):
            re = mid[i * blocks : (i + 1) * blocks, 0:lanes]
            im = mid[i * blocks : (i + 1) * blocks, lanes : 2 * lanes]
            columns.append(
                jnp.concatenate([re * twr + im * twi, im * twr - re * twi], axis=0)
            )
        out = dot3(first_back, halves(jnp.concatenate(columns, axis=1)))
        return [out[:, i * lanes : (i + 1) * lanes] for i in range(len(spectra))]

    def times(a, b):
        ar, ai = a[:, 0:lanes], a[:, lanes : 2 * lanes]
        br, bi = b[:, 0:lanes], b[:, lanes : 2 * lanes]
        return jnp.concatenate([ar * br - ai * bi, ar * bi + ai * br], axis=1)

    def conj_times(a, b):
        ar, ai = a[:, 0:lanes], a[:, lanes : 2 * lanes]
        br, bi = b[:, 0:lanes], b[:, lanes : 2 * lanes]
        return jnp.concatenate([ar * br + ai * bi, ar * bi - ai * br], axis=1)

    lane_id = lax.broadcasted_iota(jnp.int32, (blocks, lanes), 1)
    row_id = lax.broadcasted_iota(jnp.int32, (blocks, lanes), 0)

    def earlier(x):
        above = jnp.where(row_id == 0, 0.0, pltpu.roll(x, 1, 0))
        return [
            pltpu.roll(jnp.where(lane_id >= lanes - k, above, x), k, 1) for k in range(1, 3)
        ]

    def later(x):
        below = jnp.where(row_id == blocks - 1, 0.0, pltpu.roll(x, blocks - 1, 0))
        return [
            pltpu.roll(jnp.where(lane_id < k, below, x), lanes - k, 1) for k in range(1, 3)
        ]

    filters = [
        ref[pl.ds(c, count, stride=2), :] for ref in (filt1_ref, filt2_ref) for c in range(2)
    ]
    spec_f = forward(filters)
    spec_f1, spec_f2 = spec_f[0:2], spec_f[2:4]

    for d in (2, 1, 3):
        own_seq, own_cot = seq_line.at[core, mine], cot_line.at[core, mine]
        send(own_seq, own_seq, 5, 2 * line_chips[d] + core)
        send(own_cot, own_cot, 6, 2 * line_chips[d] + core)

    arrived(recv1, 0)
    stage_b[...] = recv1[...].astype(f32).reshape(count * 8, lanes)

    def tap(s, c, k):
        return taps_ref[k, width * s + 2 * me + c]

    streams = []
    for s in range(3):
        for c in range(2):
            now = stage_b[pl.ds(2 * s + c, count, stride=8), :]
            moved = [now, *earlier(now)]
            mixed = tap(s, c, 0) * now
            for k in range(1, 3):
                mixed = mixed + tap(s, c, k) * moved[k]
            streams.append(mixed.astype(bf16).astype(f32))
    value, gate_one, gate_two = streams[0:2], streams[2:4], streams[4:6]
    out_grad = [stage_b[pl.ds(6 + c, count, stride=8), :] for c in range(2)]
    grad_second_mix = [out_grad[c] * gate_two[c] for c in range(2)]

    spec = forward(value + grad_second_mix)
    spec_value, spec_gsm = spec[0:2], spec[2:4]
    mixes = backward(
        [times(spec_f1[c], spec_value[c]) for c in range(2)]
        + [conj_times(spec_f2[c], spec_gsm[c]) for c in range(2)]
    )
    first_mix, grad_first_out = mixes[0:2], mixes[2:4]
    first_out = [gate_one[c] * first_mix[c] for c in range(2)]
    grad_first_mix = [gate_one[c] * grad_first_out[c] for c in range(2)]
    spec = forward(first_out + grad_first_mix)
    spec_fo, spec_gfm = spec[0:2], spec[2:4]
    mixes = backward(
        [times(spec_f2[c], spec_fo[c]) for c in range(2)]
        + [conj_times(spec_f1[c], spec_gfm[c]) for c in range(2)]
    )
    second_mix, grad_value = mixes[0:2], mixes[2:4]
    grad_streams = (
        [g.astype(bf16).astype(f32) for g in grad_value]
        + [(grad_first_out[c] * first_mix[c]).astype(bf16).astype(f32) for c in range(2)]
        + [(out_grad[c] * second_mix[c]).astype(bf16).astype(f32) for c in range(2)]
    )
    for s in range(3):
        for c in range(2):
            g = grad_streams[2 * s + c]
            total = tap(s, c, 0) * g
            for k, moved in enumerate(later(g), 1):
                total = total + tap(s, c, k) * moved
            stage_a[pl.ds(2 * s + c, count, stride=8), :] = total
    for c in range(2):
        stage_a[pl.ds(6 + c, count, stride=8), :] = gate_two[c] * second_mix[c]
    outgoing = stage_a[...].reshape(2, SIDE * SIDE, 2, 2, 8, lanes)
    for k in range(2):
        for low in range(2):
            for high in range(2):
                send2[:, 4 * k + 2 * low + high] = outgoing[low, :, high, k].astype(bf16)
    plane_exchange(send2, recv2, 1)
    line_rest = pl.ds(0, SIDE - 1)
    arrived(seq_line.at[0, line_rest], 5)
    arrived(cot_line.at[0, line_rest], 6)
    line_to_sibling = [
        send(seq_line.at[core], seq_line.at[core], 11, sibling),
        send(cot_line.at[core], cot_line.at[core], 12, sibling),
    ]

    line = jnp.zeros((1, lanes), f32)
    short_lane = lax.broadcasted_iota(jnp.int32, (1, lanes), 1)
    for j in range(6):
        now = stage_b[pl.ds(j, count, stride=8), :]
        for k, moved in enumerate([now, *earlier(now)]):
            part = jnp.sum(grad_streams[j] * moved, axis=0, keepdims=True)
            part = jnp.sum(part, axis=1, keepdims=True)
            line = jnp.where(short_lane == 3 * j + k, part * scale, line)
    short_slab[...] = line
    grads = backward(
        [conj_times(spec_value[c], spec_gfm[c]) for c in range(2)]
        + [conj_times(spec_fo[c], spec_gsm[c]) for c in range(2)]
    )
    for c in range(2):
        gf1_ref[pl.ds(c, count, stride=2), :] = grads[c] * scale
        gf2_ref[pl.ds(c, count, stride=2), :] = grads[2 + c] * scale
    stores = [
        pltpu.make_async_copy(gf1_ref, gf1_out, out_sem.at[0]),
        pltpu.make_async_copy(gf2_ref, gf2_out, out_sem.at[1]),
    ]
    for store in stores:
        store.start()
    for copy in line_to_sibling:
        copy.wait()
    line_blocks = [(k, p) for k in range(2) for p in range(SIDE)]
    seq_all = jnp.concatenate([seq_line[k, p] for k, p in line_blocks], axis=1)
    cot_all = jnp.concatenate([cot_line[k, p] for k, p in line_blocks], axis=1)

    arrived(recv2, 1)
    rows = jnp.concatenate(
        [recv2[:, n].astype(f32).reshape(count, lanes).astype(bf16) for n in range(2 * SIDE)],
        axis=1,
    )
    with_seq = dot_nt(rows, seq_all)
    with_cot = dot_nt(rows, cot_all)
    kind = lax.broadcasted_iota(jnp.int32, (count, 256), 0) % 8
    partial = jnp.where(kind < 6, with_seq, with_cot) * scale
    send3[...] = partial.reshape(SIDE * SIDE, 8, 256).astype(bf16)
    plane_exchange(send3, recv3, 3)
    exchange(lambda peer_chip: short_slab, shorts.at[core, chip], 2)
    own_rows = rows_line.at[mine, core]
    for d in (2, 1, 3):
        for c in range(2):
            send(recv2.at[:, SIDE * c + in_line[d]], own_rows, 7, 2 * line_chips[d] + c)
    send(recv2.at[:, SIDE * (1 - core) + mine], own_rows, 7, sibling)
    pltpu.make_async_copy(recv2.at[:, SIDE * core + mine], own_rows, recv_sem.at[7]).start()

    arrived(recv3, 3)
    slab[...] = jnp.sum(recv3[...].astype(f32), axis=0).astype(bf16)
    steps = sorted(
        zip(chip_offsets(), other_chips), key=lambda item: hops(item[0]) not in VIA_SIBLING
    )
    relayed = []
    direct = 0
    own_sums = sums.at[core, chip]
    for step, peer_chip in steps:
        if hops(step) in VIA_SIBLING:
            send(slab, own_sums, 4, 2 * peer_chip + core)
            relayed.append(peer_chip)
        else:
            for c in range(2):
                send(slab, own_sums, 10, 2 * peer_chip + c)
            direct += 2
    send(slab, own_sums, 10, sibling)
    pltpu.make_async_copy(slab, own_sums, recv_sem.at[10]).start()

    arrived(shorts.at[core], 2)
    shorts_to_sibling = send(shorts.at[core], shorts.at[core], 9, sibling)
    arrived(rows_line, 7)
    by_place = [
        jnp.stack([rows_line[k, p].astype(f32) for p in range(2)], axis=1) for k in range(SIDE)
    ]
    stage_b[...] = jnp.stack(
        [jnp.stack([by_place[2 * low + high] for high in range(2)], axis=1) for low in range(2)],
        axis=0,
    ).reshape(count * 8, lanes)
    for s in range(3):
        for c in range(2):
            stage_a[pl.ds(width * s + c, count, stride=2), :] = stage_b[
                pl.ds(2 * s + c, count, stride=8), :
            ]
    grad_projected = stage_a[0 : 3 * width, :].astype(bf16)
    grad_seq = dot_tn(win_ref[...], grad_projected).astype(bf16)
    gfeat_ref[...] = dot_nt(grad_seq, pick).astype(bf16)
    stores.append(pltpu.make_async_copy(gfeat_ref, gfeat_out, out_sem.at[2]))
    stores[2].start()
    shorts_to_sibling.wait()
    for half in range(2):
        stage_a[pl.ds(half, chips, stride=2), :] = shorts[half].reshape(chips, lanes)
    by_owner = stage_a[0:count, :]
    owner = lax.broadcasted_iota(jnp.int32, (count, width), 0)
    column = lax.broadcasted_iota(jnp.int32, (count, width), 1)
    spread = [
        lax.dot_general(
            by_owner,
            jnp.where(column == 2 * owner + c, 1.0, 0.0),
            (((0,), (0,)), ((), ())),
            preferred_element_type=f32,
            precision=lax.Precision.HIGHEST,
        )
        for c in range(2)
    ]
    for s in range(3):
        gshort_ref[:, width * s : width * (s + 1)] = (
            spread[0][6 * s : 6 * s + 3, :] + spread[1][6 * s + 3 : 6 * s + 6, :]
        )
    stores.append(pltpu.make_async_copy(gshort_ref, short_out, out_sem.at[3]))
    stores[3].start()

    relayed_slots = sums.at[0, pl.ds(0, len(relayed))]
    arrived(relayed_slots, 4)
    for peer_chip in relayed:
        send(sums.at[core, peer_chip], sums.at[core, peer_chip], 8, sibling)
    sent(send1.at[pl.ds(0, count - 1)], 0)
    sent(seq_line.at[0, line_rest], 5)
    sent(cot_line.at[0, line_rest], 6)
    sent(shorts.at[0, pl.ds(0, chips - 1)], 2)
    place_rest = pl.ds(0, SIDE * SIDE - 1)
    sent(send2.at[place_rest], 1)
    sent(send3.at[place_rest], 3)
    sent(recv1.at[pl.ds(0, count - SIDE * SIDE)], 7)
    arrived(sums.at[0, pl.ds(0, direct + 2)], 10)
    arrived(relayed_slots, 8)
    sent(relayed_slots, 4)
    sent(sums.at[0, pl.ds(0, direct + 1)], 10)
    sent(relayed_slots, 8)
    for store in stores:
        store.wait()


def finish_kernel(
    count,
    sums_in,
    short_in,
    gfeat_in,
    gf1_in,
    gf2_in,
    gfeat_out,
    gwin_out,
    gwout_out,
    gshort_out,
    gf1_out,
    gf2_out,
    sums_ref,
    gfeat_ref,
    gf1_ref,
    gf2_ref,
    gwout_ref,
    gshort_ref,
    ordered,
    stage,
    in_sem,
    out_sem,
):
    chips = count // 2
    lanes = 128
    width = 2 * count
    loads = [
        pltpu.make_async_copy(source, target, in_sem.at[n])
        for n, (source, target) in enumerate(
            (
                (sums_in.at[:, :, :, pl.ds(0, lanes)], sums_ref.at[0]),
                (sums_in.at[:, :, :, pl.ds(lanes, lanes)], sums_ref.at[1]),
                (short_in, gshort_ref),
                (gf1_in, gf1_ref),
                (gf2_in, gf2_ref),
                (gfeat_in, gfeat_ref),
            )
        )
    ]
    for load in loads:
        load.start()
    stores = []

    def store(source, target):
        copy = pltpu.make_async_copy(source, target, out_sem.at[len(stores)])
        copy.start()
        stores.append(copy)

    for h in range(2):
        loads[h].wait()
        part = pl.ds(h * lanes, lanes)
        stage[...] = sums_ref[h].astype(f32).reshape(count * 8, lanes)
        for half in range(2):
            for s in range(4):
                for c in range(2):
                    ordered[h, pl.ds(width * s + 2 * half + c, chips, stride=4), :] = stage[
                        pl.ds(chips * 8 * half + 2 * s + c, chips, stride=8), :
                    ]
        store(ordered.at[h, pl.ds(0, 3 * width)], gwin_out.at[:, part])
        gwout_ref[part, :] = ordered[h, 3 * width : 4 * width, :].T
        store(gwout_ref.at[part], gwout_out.at[part])
    for n, (ref, target) in enumerate(((gf1_ref, gf1_out), (gf2_ref, gf2_out), (gfeat_ref, gfeat_out))):
        loads[3 + n].wait()
        store(ref, target)
    loads[2].wait()
    store(gshort_ref, gshort_out)
    for copy in stores:
        copy.wait()


def local(
    count, features, sink_order, cotangent, w_in, short_taps, w_out, filter_one, filter_two
):
    width, lanes = features.shape
    length = filter_one.shape[1]
    chips = count // 2
    tables, twiddle = (jnp.asarray(t) for t in transform_tables(count, lanes))

    def by_row(filt):
        return filt.reshape(2, count, lanes).transpose(1, 0, 2).reshape(2 * count, lanes)

    def by_channel(grad):
        return grad.reshape(count, 2, lanes).transpose(1, 0, 2).reshape(2, length)

    anywhere = pl.BlockSpec(memory_space=pl.ANY)
    shape = jax.ShapeDtypeStruct
    grad_shapes = (
        shape((width, lanes), bf16),
        shape((width, lanes), f32),
        shape((width, lanes), f32),
    )
    sums, shorts, gfeat, gf1, gf2 = pl.pallas_call(
        functools.partial(kernel, count),
        out_shape=(
            shape((2, chips, 8, width), bf16),
            shape((3, 3 * width), f32),
            *grad_shapes,
        ),
        in_specs=[anywhere] * 10,
        out_specs=(anywhere,) * 5,
        scratch_shapes=[
            pltpu.VMEM((width, lanes), bf16),
            pltpu.VMEM((1, lanes), jnp.int32),
            pltpu.VMEM((2, SIDE, width, lanes), bf16),
            pltpu.VMEM((3 * width, width), bf16),
            pltpu.VMEM((width, width), bf16),
            pltpu.SMEM((3, 3 * width), f32),
            pltpu.VMEM((width, lanes), f32),
            pltpu.VMEM((width, lanes), f32),
            pltpu.VMEM(tables.shape, bf16),
            pltpu.VMEM(twiddle.shape, f32),
            pltpu.VMEM((width, lanes), bf16),
            pltpu.VMEM((width, lanes), f32),
            pltpu.VMEM((width, lanes), f32),
            pltpu.VMEM((3, 3 * width), f32),
            pltpu.VMEM((8 * count, lanes), f32),
            pltpu.VMEM((8 * count, lanes), f32),
            pltpu.VMEM((2, SIDE, width, lanes), bf16),
            pltpu.VMEM((count, 8, lanes), bf16),
            pltpu.VMEM((count, 8, lanes), bf16),
            pltpu.VMEM((SIDE * SIDE, 2 * SIDE, 8, lanes), bf16),
            pltpu.VMEM((SIDE * SIDE, 2 * SIDE, 8, lanes), bf16),
            pltpu.VMEM((SIDE, 2, SIDE * SIDE, 8, lanes), bf16),
            pltpu.VMEM((SIDE * SIDE, 8, width), bf16),
            pltpu.VMEM((SIDE * SIDE, 8, width), bf16),
            pltpu.VMEM((8, width), bf16),
            pltpu.VMEM((1, lanes), f32),
            pltpu.VMEM((2, chips, 1, lanes), f32),
            pltpu.SemaphoreType.DMA((10,)),
            pltpu.SemaphoreType.DMA((5,)),
            pltpu.SemaphoreType.DMA((13,)),
            pltpu.SemaphoreType.DMA((13,)),
            pltpu.SemaphoreType.REGULAR,
        ],
        compiler_params=pltpu.CompilerParams(collective_id=0, has_side_effects=True),
        name="hyena_backward",
    )(
        features,
        sink_order,
        cotangent,
        w_in,
        w_out,
        short_taps.T,
        by_row(filter_one),
        by_row(filter_two),
        tables,
        twiddle,
    )
    gfeat, gwin, gwout, gshort, gf1, gf2 = pl.pallas_call(
        functools.partial(finish_kernel, count),
        out_shape=(
            grad_shapes[0],
            shape((3 * width, width), f32),
            shape((width, width), f32),
            shape((3, 3 * width), f32),
            *grad_shapes[1:],
        ),
        in_specs=[anywhere] * 5,
        out_specs=(anywhere,) * 6,
        scratch_shapes=[
            pltpu.VMEM((2, 2, chips, 8, lanes), bf16),
            pltpu.VMEM((width, lanes), bf16),
            pltpu.VMEM((width, lanes), f32),
            pltpu.VMEM((width, lanes), f32),
            pltpu.VMEM((width, width), f32),
            pltpu.VMEM((3, 3 * width), f32),
            pltpu.VMEM((2, 8 * count, lanes), f32),
            pltpu.VMEM((8 * count, lanes), f32),
            pltpu.SemaphoreType.DMA((6,)),
            pltpu.SemaphoreType.DMA((8,)),
        ],
        name="row_order",
    )(sums, shorts, gfeat, gf1, gf2)
    return gfeat, gwin, gwout, gshort.T, by_channel(gf1), by_channel(gf2)


def solution(mesh):
    count = mesh.shape["seq"] * mesh.shape["fft"]
    both = ("seq", "fft")
    return jax.shard_map(
        functools.partial(local, count),
        mesh=mesh,
        in_specs=(
            P(None, both),
            P(both, None),
            P(None, both),
            P(),
            P(),
            P(),
            P(both, None),
            P(both, None),
        ),
        out_specs=(P(None, both), P(), P(), P(), P(both, None), P(both, None)),
        check_vma=False,
    )
```

```python
import functools
import math

import jax
import jax.numpy as jnp
import ml_dtypes
import numpy as np
from jax import lax
from jax.experimental import pallas as pl
from jax.experimental.pallas import tpu as pltpu
from jax.sharding import PartitionSpec as P

bf16 = jnp.bfloat16
f32 = jnp.float32
LOGICAL = pl.DeviceIdType.LOGICAL
SIDE = 4
VIA_SIBLING = (3, 4)


def hops(step):
    return sum(min(d, SIDE - d) for d in step)


def chip_offsets():
    steps = [(a, b, c) for a in range(SIDE) for b in range(SIDE) for c in range(SIDE) if a + b + c]
    return sorted(steps, key=lambda step: (-hops(step), tuple(-min(d, SIDE - d) for d in step)))


def plane_offsets():
    return [step for step in chip_offsets() if step[0] == 0]


def table_halves(table):
    high = table.astype(ml_dtypes.bfloat16)
    low = (table - high.astype(np.float64)).astype(ml_dtypes.bfloat16)
    return high, low


def transform_tables(blocks, lanes):
    length = blocks * lanes
    shift = 0.25
    row = np.arange(blocks, dtype=np.float64)
    lane = np.arange(lanes, dtype=np.float64)
    outer = -2.0 * np.pi * np.outer(row + shift, row) / blocks
    twist = -2.0 * np.pi * np.outer(row + shift, lane) / length
    inner = -2.0 * np.pi * (np.outer(lane, lane) % lanes) / lanes
    first = np.concatenate([np.cos(outer), np.sin(outer)], axis=0)
    second = np.block(
        [[np.cos(inner), np.sin(inner)], [-np.sin(inner), np.cos(inner)]]
    )
    second_back = second.T
    first_back = np.concatenate([np.cos(outer).T, np.sin(outer).T], axis=1) / length
    twiddle = np.concatenate([np.cos(twist), np.sin(twist)], axis=1).astype(np.float32)
    pieces = [np.concatenate(table_halves(first), axis=1)]
    for table in (second, second_back, first_back):
        pieces.extend(table_halves(table))
    return np.concatenate(pieces, axis=0), twiddle


def halves(x):
    high = x.astype(bf16)
    return high, (x - high.astype(f32)).astype(bf16)


def dot(a, b):
    return jnp.dot(a, b, preferred_element_type=f32)


def dot_nt(a, b):
    return lax.dot_general(a, b, (((1,), (1,)), ((), ())), preferred_element_type=f32)


def dot_tn(a, b):
    return lax.dot_general(a, b, (((0,), (0,)), ((), ())), preferred_element_type=f32)


def dot3(left, right):
    return dot(left[0], right[0]) + (dot(left[0], right[1]) + dot(left[1], right[0]))


def kernel(
    count,
    feat_in,
    order_in,
    cot_in,
    win_in,
    wout_in,
    taps_in,
    filt1_in,
    filt2_in,
    tab_in,
    tw_in,
    sums,
    short_out,
    gfeat_out,
    gf1_out,
    gf2_out,
    feat_ref,
    order_ref,
    cot_line,
    win_ref,
    wout_ref,
    taps_ref,
    filt1_ref,
    filt2_ref,
    tab_ref,
    tw_ref,
    gfeat_ref,
    gf1_ref,
    gf2_ref,
    gshort_ref,
    stage_a,
    stage_b,
    seq_line,
    send1,
    recv1,
    send2,
    recv2,
    rows_line,
    send3,
    recv3,
    slab,
    short_slab,
    shorts,
    in_sem,
    out_sem,
    send_sem,
    recv_sem,
    ready_sem,
):
    blocks = count
    chips = count // 2
    lanes = 128
    width = 2 * count
    scale = 1.0 / math.sqrt(blocks * lanes)

    seq_index = lax.axis_index("seq")
    fft_index = lax.axis_index("fft")
    core = lax.rem(fft_index, 2)
    x = lax.rem(lax.div(fft_index, 2), 2) * 2 + lax.div(seq_index, SIDE)
    y = lax.div(fft_index, SIDE)
    z = lax.rem(seq_index, SIDE)
    turned_x, turned_y, turned_z = ([lax.rem(p + d, SIDE) for d in range(SIDE)] for p in (x, y, z))
    along_x = [lax.rem(p, 2) * 32 + lax.div(p, 2) for p in turned_x]
    along_y = [p * 2 for p in turned_y]
    along_z = [p * 8 for p in turned_z]
    chip = along_x[0] + along_y[0] + along_z[0]
    me = 2 * chip + core
    sibling = 2 * chip + (1 - core)
    other_chips = [along_x[a] + along_y[b] + along_z[c] for a, b, c in chip_offsets()]
    in_line = [lax.rem(p, 2) * 2 + lax.div(p, 2) for p in turned_x]
    line_chips = [along_x[d] + along_y[0] + along_z[0] for d in range(SIDE)]
    here = z * SIDE + y
    plane = [
        (turned_z[c] * SIDE + turned_y[b], along_x[0] + along_y[b] + along_z[c])
        for _, b, c in plane_offsets()
    ]
    mine = in_line[0]

    barrier = pltpu.get_barrier_semaphore()
    for peer_chip in other_chips:
        pl.semaphore_signal(
            barrier, inc=1, device_id=2 * peer_chip + core, device_id_type=LOGICAL
        )
    pl.semaphore_signal(barrier, inc=1, device_id=sibling, device_id_type=LOGICAL)
    loads = [
        pltpu.make_async_copy(source, target, in_sem.at[n])
        for n, (source, target) in enumerate(
            (
                (feat_in, feat_ref),
                (order_in, order_ref),
                (cot_in, cot_line.at[core, mine]),
                (win_in, win_ref),
                (wout_in, wout_ref),
                (taps_in, taps_ref),
                (filt1_in, filt1_ref),
                (filt2_in, filt2_ref),
                (tab_in, tab_ref),
                (tw_in, tw_ref),
            )
        )
    ]
    for load in loads:
        load.start()

    def send(source, target, phase, peer):
        copy = pltpu.make_async_remote_copy(
            source,
            target,
            send_sem.at[phase],
            recv_sem.at[phase],
            device_id=peer,
            device_id_type=LOGICAL,
        )
        copy.start()
        return copy

    def exchange(source, target, phase):
        for peer_chip in other_chips:
            send(source(peer_chip), target, phase, 2 * peer_chip + core)
        pltpu.make_async_copy(source(chip), target, recv_sem.at[phase]).start()

    def arrived(whole, phase):
        pltpu.make_async_copy(whole, whole, recv_sem.at[phase]).wait()

    def plane_exchange(source, target, phase):
        for place, peer_chip in plane:
            send(source.at[place], target.at[here], phase, 2 * peer_chip + core)
        pltpu.make_async_copy(source.at[here], target.at[here], recv_sem.at[phase]).start()

    def sent(part, phase):
        pltpu.make_async_copy(part, part, send_sem.at[phase]).wait()

    for n in range(5):
        loads[n].wait()
    order = order_ref[...]
    pick = jnp.where(
        lax.broadcasted_iota(jnp.int32, (lanes, lanes), 0) == order, 1.0, 0.0
    ).astype(bf16)
    seq_input = dot(feat_ref[...], pick).astype(bf16)
    seq_line[core, mine] = seq_input
    stage_a[0 : 3 * width, :] = dot(win_ref[...], seq_input)
    stage_a[3 * width : 4 * width, :] = dot_tn(wout_ref[...], cot_line[core, mine])
    for s in range(4):
        for c in range(2):
            stage_b[pl.ds(2 * s + c, count, stride=8), :] = stage_a[
                pl.ds(width * s + c, count, stride=2), :
            ]
    send1[...] = stage_b[...].reshape(count, 8, lanes).astype(bf16)

    pl.semaphore_wait(barrier, chips)
    pl.semaphore_signal(ready_sem, inc=1, device_id=sibling, device_id_type=LOGICAL)
    pl.semaphore_wait(ready_sem, 1)
    for peer_chip in other_chips:
        for c in range(2):
            peer = 2 * peer_chip + c
            send(send1.at[peer], recv1.at[me], 0, peer)
    send(send1.at[sibling], recv1.at[me], 0, sibling)
    pltpu.make_async_copy(send1.at[me], recv1.at[me], recv_sem.at[0]).start()

    for n in range(5, 10):
        loads[n].wait()
    twr = tw_ref[:, 0:lanes]
    twi = tw_ref[:, lanes : 2 * lanes]
    first = tab_ref[0:256, :]
    second = (tab_ref[256:512, :], tab_ref[512:768, :])
    second_back = (tab_ref[768:1024, :], tab_ref[1024:1280, :])
    first_back = (tab_ref[1280:1408, :], tab_ref[1408:1536, :])

    def forward(signals, exact=0):
        high, low = halves(jnp.concatenate(signals, axis=1))
        mid = dot(first, jnp.concatenate([high, high], axis=0))
        rest = exact * lanes
        tail = mid[:, rest:] + dot(first[:, 0:lanes], low[:, rest:])
        mid = jnp.concatenate([mid[:, 0:rest], tail], axis=1) if exact else tail
        rows = []
        for i in range(len(signals)):
            re = mid[0:blocks, i * lanes : (i + 1) * lanes]
            im = mid[blocks : 2 * blocks, i * lanes : (i + 1) * lanes]
            rows.append(
                jnp.concatenate([re * twr - im * twi, re * twi + im * twr], axis=1)
            )
        out = dot3(halves(jnp.concatenate(rows, axis=0)), second)
        return [out[i * blocks : (i + 1) * blocks, :] for i in range(len(signals))]

    def backward(spectra):
        mid = dot3(halves(jnp.concatenate(spectra, axis=0)), second_back)
        columns = []
        for i in range(len(spectra)):
            re = mid[i * blocks : (i + 1) * blocks, 0:lanes]
            im = mid[i * blocks : (i + 1) * blocks, lanes : 2 * lanes]
            columns.append(
                jnp.concatenate([re * twr + im * twi, im * twr - re * twi], axis=0)
            )
        out = dot3(first_back, halves(jnp.concatenate(columns, axis=1)))
        return [out[:, i * lanes : (i + 1) * lanes] for i in range(len(spectra))]

    def times(a, b):
        ar, ai = a[:, 0:lanes], a[:, lanes : 2 * lanes]
        br, bi = b[:, 0:lanes], b[:, lanes : 2 * lanes]
        return jnp.concatenate([ar * br - ai * bi, ar * bi + ai * br], axis=1)

    def conj_times(a, b):
        ar, ai = a[:, 0:lanes], a[:, lanes : 2 * lanes]
        br, bi = b[:, 0:lanes], b[:, lanes : 2 * lanes]
        return jnp.concatenate([ar * br + ai * bi, ar * bi - ai * br], axis=1)

    lane_id = lax.broadcasted_iota(jnp.int32, (blocks, lanes), 1)
    row_id = lax.broadcasted_iota(jnp.int32, (blocks, lanes), 0)

    def earlier(x):
        above = jnp.where(row_id == 0, 0.0, pltpu.roll(x, 1, 0))
        return [
            pltpu.roll(jnp.where(lane_id >= lanes - k, above, x), k, 1) for k in range(1, 3)
        ]

    def later(x):
        below = jnp.where(row_id == blocks - 1, 0.0, pltpu.roll(x, blocks - 1, 0))
        return [
            pltpu.roll(jnp.where(lane_id < k, below, x), lanes - k, 1) for k in range(1, 3)
        ]

    filters = [
        ref[pl.ds(c, count, stride=2), :] for ref in (filt1_ref, filt2_ref) for c in range(2)
    ]
    spec_f = forward(filters)
    spec_f1, spec_f2 = spec_f[0:2], spec_f[2:4]

    for d in (2, 1, 3):
        own_seq, own_cot = seq_line.at[core, mine], cot_line.at[core, mine]
        send(own_seq, own_seq, 5, 2 * line_chips[d] + core)
        send(own_cot, own_cot, 6, 2 * line_chips[d] + core)

    arrived(recv1, 0)
    stage_b[...] = recv1[...].astype(f32).reshape(count * 8, lanes)

    def tap(s, c, k):
        return taps_ref[k, width * s + 2 * me + c]

    streams = []
    for s in range(3):
        for c in range(2):
            now = stage_b[pl.ds(2 * s + c, count, stride=8), :]
            moved = [now, *earlier(now)]
            mixed = tap(s, c, 0) * now
            for k in range(1, 3):
                mixed = mixed + tap(s, c, k) * moved[k]
            streams.append(mixed.astype(bf16).astype(f32))
    value, gate_one, gate_two = streams[0:2], streams[2:4], streams[4:6]
    out_grad = [stage_b[pl.ds(6 + c, count, stride=8), :] for c in range(2)]
    grad_second_mix = [out_grad[c] * gate_two[c] for c in range(2)]

    spec = forward(value + grad_second_mix, exact=2)
    spec_value, spec_gsm = spec[0:2], spec[2:4]
    mixes = backward(
        [times(spec_f1[c], spec_value[c]) for c in range(2)]
        + [conj_times(spec_f2[c], spec_gsm[c]) for c in range(2)]
    )
    first_mix, grad_first_out = mixes[0:2], mixes[2:4]
    first_out = [gate_one[c] * first_mix[c] for c in range(2)]
    grad_first_mix = [gate_one[c] * grad_first_out[c] for c in range(2)]
    spec = forward(first_out + grad_first_mix)
    spec_fo, spec_gfm = spec[0:2], spec[2:4]
    mixes = backward(
        [times(spec_f2[c], spec_fo[c]) for c in range(2)]
        + [conj_times(spec_f1[c], spec_gfm[c]) for c in range(2)]
    )
    second_mix, grad_value = mixes[0:2], mixes[2:4]
    grad_streams = (
        [g.astype(bf16).astype(f32) for g in grad_value]
        + [(grad_first_out[c] * first_mix[c]).astype(bf16).astype(f32) for c in range(2)]
        + [(out_grad[c] * second_mix[c]).astype(bf16).astype(f32) for c in range(2)]
    )
    for s in range(3):
        for c in range(2):
            g = grad_streams[2 * s + c]
            total = tap(s, c, 0) * g
            for k, moved in enumerate(later(g), 1):
                total = total + tap(s, c, k) * moved
            stage_a[pl.ds(2 * s + c, count, stride=8), :] = total
    for c in range(2):
        stage_a[pl.ds(6 + c, count, stride=8), :] = gate_two[c] * second_mix[c]
    outgoing = stage_a[...].reshape(2, SIDE * SIDE, 2, 2, 8, lanes)
    for k in range(2):
        for low in range(2):
            for high in range(2):
                send2[:, 4 * k + 2 * low + high] = outgoing[low, :, high, k].astype(bf16)
    plane_exchange(send2, recv2, 1)
    line_rest = pl.ds(0, SIDE - 1)
    arrived(seq_line.at[0, line_rest], 5)
    arrived(cot_line.at[0, line_rest], 6)
    line_to_sibling = [
        send(seq_line.at[core], seq_line.at[core], 11, sibling),
        send(cot_line.at[core], cot_line.at[core], 12, sibling),
    ]

    line = jnp.zeros((1, lanes), f32)
    short_lane = lax.broadcasted_iota(jnp.int32, (1, lanes), 1)
    for j in range(6):
        now = stage_b[pl.ds(j, count, stride=8), :]
        for k, moved in enumerate([now, *earlier(now)]):
            part = jnp.sum(grad_streams[j] * moved, axis=0, keepdims=True)
            part = jnp.sum(part, axis=1, keepdims=True)
            line = jnp.where(short_lane == 3 * j + k, part * scale, line)
    short_slab[...] = line
    grads = backward(
        [conj_times(spec_value[c], spec_gfm[c]) for c in range(2)]
        + [conj_times(spec_fo[c], spec_gsm[c]) for c in range(2)]
    )
    for c in range(2):
        gf1_ref[pl.ds(c, count, stride=2), :] = grads[c] * scale
        gf2_ref[pl.ds(c, count, stride=2), :] = grads[2 + c] * scale
    stores = [
        pltpu.make_async_copy(gf1_ref, gf1_out, out_sem.at[0]),
        pltpu.make_async_copy(gf2_ref, gf2_out, out_sem.at[1]),
    ]
    for store in stores:
        store.start()
    for copy in line_to_sibling:
        copy.wait()
    line_blocks = [(k, p) for k in range(2) for p in range(SIDE)]
    seq_all = jnp.concatenate([seq_line[k, p] for k, p in line_blocks], axis=1)
    cot_all = jnp.concatenate([cot_line[k, p] for k, p in line_blocks], axis=1)

    arrived(recv2, 1)
    rows = jnp.concatenate(
        [recv2[:, n].astype(f32).reshape(count, lanes).astype(bf16) for n in range(2 * SIDE)],
        axis=1,
    )
    with_seq = dot_nt(rows, seq_all)
    with_cot = dot_nt(rows, cot_all)
    kind = lax.broadcasted_iota(jnp.int32, (count, 256), 0) % 8
    partial = jnp.where(kind < 6, with_seq, with_cot) * scale
    send3[...] = partial.reshape(SIDE * SIDE, 8, 256).astype(bf16)
    plane_exchange(send3, recv3, 3)
    exchange(lambda peer_chip: short_slab, shorts.at[core, chip], 2)
    own_rows = rows_line.at[mine, core]
    for d in (2, 1, 3):
        for c in range(2):
            send(recv2.at[:, SIDE * c + in_line[d]], own_rows, 7, 2 * line_chips[d] + c)
    send(recv2.at[:, SIDE * (1 - core) + mine], own_rows, 7, sibling)
    pltpu.make_async_copy(recv2.at[:, SIDE * core + mine], own_rows, recv_sem.at[7]).start()

    arrived(recv3, 3)
    slab[...] = jnp.sum(recv3[...].astype(f32), axis=0).astype(bf16)
    steps = sorted(
        zip(chip_offsets(), other_chips), key=lambda item: hops(item[0]) not in VIA_SIBLING
    )
    relayed = []
    direct = 0
    own_sums = sums.at[core, chip]
    for step, peer_chip in steps:
        if hops(step) in VIA_SIBLING:
            send(slab, own_sums, 4, 2 * peer_chip + core)
            relayed.append(peer_chip)
        else:
            for c in range(2):
                send(slab, own_sums, 10, 2 * peer_chip + c)
            direct += 2
    send(slab, own_sums, 10, sibling)
    pltpu.make_async_copy(slab, own_sums, recv_sem.at[10]).start()

    arrived(shorts.at[core], 2)
    shorts_to_sibling = send(shorts.at[core], shorts.at[core], 9, sibling)
    arrived(rows_line, 7)
    by_place = [
        jnp.stack([rows_line[k, p].astype(f32) for p in range(2)], axis=1) for k in range(SIDE)
    ]
    stage_b[...] = jnp.stack(
        [jnp.stack([by_place[2 * low + high] for high in range(2)], axis=1) for low in range(2)],
        axis=0,
    ).reshape(count * 8, lanes)
    for s in range(3):
        for c in range(2):
            stage_a[pl.ds(width * s + c, count, stride=2), :] = stage_b[
                pl.ds(2 * s + c, count, stride=8), :
            ]
    grad_projected = stage_a[0 : 3 * width, :].astype(bf16)
    grad_seq = dot_tn(win_ref[...], grad_projected).astype(bf16)
    gfeat_ref[...] = dot_nt(grad_seq, pick).astype(bf16)
    stores.append(pltpu.make_async_copy(gfeat_ref, gfeat_out, out_sem.at[2]))
    stores[2].start()
    shorts_to_sibling.wait()
    for half in range(2):
        stage_a[pl.ds(half, chips, stride=2), :] = shorts[half].reshape(chips, lanes)
    by_owner = stage_a[0:count, :]
    owner = lax.broadcasted_iota(jnp.int32, (count, width), 0)
    column = lax.broadcasted_iota(jnp.int32, (count, width), 1)
    spread = [
        lax.dot_general(
            by_owner,
            jnp.where(column == 2 * owner + c, 1.0, 0.0),
            (((0,), (0,)), ((), ())),
            preferred_element_type=f32,
            precision=lax.Precision.HIGHEST,
        )
        for c in range(2)
    ]
    for s in range(3):
        gshort_ref[:, width * s : width * (s + 1)] = (
            spread[0][6 * s : 6 * s + 3, :] + spread[1][6 * s + 3 : 6 * s + 6, :]
        )
    stores.append(pltpu.make_async_copy(gshort_ref, short_out, out_sem.at[3]))
    stores[3].start()

    relayed_slots = sums.at[0, pl.ds(0, len(relayed))]
    arrived(relayed_slots, 4)
    for peer_chip in relayed:
        send(sums.at[core, peer_chip], sums.at[core, peer_chip], 8, sibling)
    sent(send1.at[pl.ds(0, count - 1)], 0)
    sent(seq_line.at[0, line_rest], 5)
    sent(cot_line.at[0, line_rest], 6)
    sent(shorts.at[0, pl.ds(0, chips - 1)], 2)
    place_rest = pl.ds(0, SIDE * SIDE - 1)
    sent(send2.at[place_rest], 1)
    sent(send3.at[place_rest], 3)
    sent(recv1.at[pl.ds(0, count - SIDE * SIDE)], 7)
    arrived(sums.at[0, pl.ds(0, direct + 2)], 10)
    arrived(relayed_slots, 8)
    sent(relayed_slots, 4)
    sent(sums.at[0, pl.ds(0, direct + 1)], 10)
    sent(relayed_slots, 8)
    for store in stores:
        store.wait()


def finish_kernel(
    count,
    sums_in,
    short_in,
    gfeat_in,
    gf1_in,
    gf2_in,
    gfeat_out,
    gwin_out,
    gwout_out,
    gshort_out,
    gf1_out,
    gf2_out,
    sums_ref,
    gfeat_ref,
    gf1_ref,
    gf2_ref,
    gwout_ref,
    gshort_ref,
    ordered,
    stage,
    in_sem,
    out_sem,
):
    chips = count // 2
    lanes = 128
    width = 2 * count
    loads = [
        pltpu.make_async_copy(source, target, in_sem.at[n])
        for n, (source, target) in enumerate(
            (
                (sums_in.at[:, :, :, pl.ds(0, lanes)], sums_ref.at[0]),
                (sums_in.at[:, :, :, pl.ds(lanes, lanes)], sums_ref.at[1]),
                (short_in, gshort_ref),
                (gf1_in, gf1_ref),
                (gf2_in, gf2_ref),
                (gfeat_in, gfeat_ref),
            )
        )
    ]
    for load in loads:
        load.start()
    stores = []

    def store(source, target):
        copy = pltpu.make_async_copy(source, target, out_sem.at[len(stores)])
        copy.start()
        stores.append(copy)

    for h in range(2):
        loads[h].wait()
        part = pl.ds(h * lanes, lanes)
        stage[...] = sums_ref[h].astype(f32).reshape(count * 8, lanes)
        for half in range(2):
            for s in range(4):
                for c in range(2):
                    ordered[h, pl.ds(width * s + 2 * half + c, chips, stride=4), :] = stage[
                        pl.ds(chips * 8 * half + 2 * s + c, chips, stride=8), :
                    ]
        store(ordered.at[h, pl.ds(0, 3 * width)], gwin_out.at[:, part])
        gwout_ref[part, :] = ordered[h, 3 * width : 4 * width, :].T
        store(gwout_ref.at[part], gwout_out.at[part])
    for n, (ref, target) in enumerate(((gf1_ref, gf1_out), (gf2_ref, gf2_out), (gfeat_ref, gfeat_out))):
        loads[3 + n].wait()
        store(ref, target)
    loads[2].wait()
    store(gshort_ref, gshort_out)
    for copy in stores:
        copy.wait()


def local(
    count, features, sink_order, cotangent, w_in, short_taps, w_out, filter_one, filter_two
):
    width, lanes = features.shape
    length = filter_one.shape[1]
    chips = count // 2
    tables, twiddle = (jnp.asarray(t) for t in transform_tables(count, lanes))

    def by_row(filt):
        return filt.reshape(2, count, lanes).transpose(1, 0, 2).reshape(2 * count, lanes)

    def by_channel(grad):
        return grad.reshape(count, 2, lanes).transpose(1, 0, 2).reshape(2, length)

    anywhere = pl.BlockSpec(memory_space=pl.ANY)
    shape = jax.ShapeDtypeStruct
    grad_shapes = (
        shape((width, lanes), bf16),
        shape((width, lanes), f32),
        shape((width, lanes), f32),
    )
    sums, shorts, gfeat, gf1, gf2 = pl.pallas_call(
        functools.partial(kernel, count),
        out_shape=(
            shape((2, chips, 8, width), bf16),
            shape((3, 3 * width), f32),
            *grad_shapes,
        ),
        in_specs=[anywhere] * 10,
        out_specs=(anywhere,) * 5,
        scratch_shapes=[
            pltpu.VMEM((width, lanes), bf16),
            pltpu.VMEM((1, lanes), jnp.int32),
            pltpu.VMEM((2, SIDE, width, lanes), bf16),
            pltpu.VMEM((3 * width, width), bf16),
            pltpu.VMEM((width, width), bf16),
            pltpu.SMEM((3, 3 * width), f32),
            pltpu.VMEM((width, lanes), f32),
            pltpu.VMEM((width, lanes), f32),
            pltpu.VMEM(tables.shape, bf16),
            pltpu.VMEM(twiddle.shape, f32),
            pltpu.VMEM((width, lanes), bf16),
            pltpu.VMEM((width, lanes), f32),
            pltpu.VMEM((width, lanes), f32),
            pltpu.VMEM((3, 3 * width), f32),
            pltpu.VMEM((8 * count, lanes), f32),
            pltpu.VMEM((8 * count, lanes), f32),
            pltpu.VMEM((2, SIDE, width, lanes), bf16),
            pltpu.VMEM((count, 8, lanes), bf16),
            pltpu.VMEM((count, 8, lanes), bf16),
            pltpu.VMEM((SIDE * SIDE, 2 * SIDE, 8, lanes), bf16),
            pltpu.VMEM((SIDE * SIDE, 2 * SIDE, 8, lanes), bf16),
            pltpu.VMEM((SIDE, 2, SIDE * SIDE, 8, lanes), bf16),
            pltpu.VMEM((SIDE * SIDE, 8, width), bf16),
            pltpu.VMEM((SIDE * SIDE, 8, width), bf16),
            pltpu.VMEM((8, width), bf16),
            pltpu.VMEM((1, lanes), f32),
            pltpu.VMEM((2, chips, 1, lanes), f32),
            pltpu.SemaphoreType.DMA((10,)),
            pltpu.SemaphoreType.DMA((5,)),
            pltpu.SemaphoreType.DMA((13,)),
            pltpu.SemaphoreType.DMA((13,)),
            pltpu.SemaphoreType.REGULAR,
        ],
        compiler_params=pltpu.CompilerParams(collective_id=0, has_side_effects=True),
        name="hyena_backward",
    )(
        features,
        sink_order,
        cotangent,
        w_in,
        w_out,
        short_taps.T,
        by_row(filter_one),
        by_row(filter_two),
        tables,
        twiddle,
    )
    gfeat, gwin, gwout, gshort, gf1, gf2 = pl.pallas_call(
        functools.partial(finish_kernel, count),
        out_shape=(
            grad_shapes[0],
            shape((3 * width, width), f32),
            shape((width, width), f32),
            shape((3, 3 * width), f32),
            *grad_shapes[1:],
        ),
        in_specs=[anywhere] * 5,
        out_specs=(anywhere,) * 6,
        scratch_shapes=[
            pltpu.VMEM((2, 2, chips, 8, lanes), bf16),
            pltpu.VMEM((width, lanes), bf16),
            pltpu.VMEM((width, lanes), f32),
            pltpu.VMEM((width, lanes), f32),
            pltpu.VMEM((width, width), f32),
            pltpu.VMEM((3, 3 * width), f32),
            pltpu.VMEM((2, 8 * count, lanes), f32),
            pltpu.VMEM((8 * count, lanes), f32),
            pltpu.SemaphoreType.DMA((6,)),
            pltpu.SemaphoreType.DMA((8,)),
        ],
        name="row_order",
    )(sums, shorts, gfeat, gf1, gf2)
    return gfeat, gwin, gwout, gshort.T, by_channel(gf1), by_channel(gf2)


def solution(mesh):
    count = mesh.shape["seq"] * mesh.shape["fft"]
    both = ("seq", "fft")
    return jax.shard_map(
        functools.partial(local, count),
        mesh=mesh,
        in_specs=(
            P(None, both),
            P(both, None),
            P(None, both),
            P(),
            P(),
            P(),
            P(both, None),
            P(both, None),
        ),
        out_specs=(P(None, both), P(), P(), P(), P(both, None), P(both, None)),
        check_vma=False,
    )
```
